32 devices in a mesh: elem: 8 (over y, x, core), mode: 4 (over z).
Axes of the slice: x: 2, y: 2, z: 4, core: 2. Of those that a mesh axis runs over, the one named last changes fastest.
Arguments:
- velocity: float32 [3, 5184, 2, 512], P(None, 'elem', None, 'mode'), may hold values from -3 to 3
- column_width: float32 [8], P('elem'), may hold values from 0.5 to 2
- row_height: float32 [8], replicated, may hold values from 0.5 to 2
- disc_mask: int32 [64], P('elem'), may hold values from 0 to 1, as said below
Outputs:
- velocity_new: float32 [3, 5184, 2, 512], P(None, 'elem', None, 'mode')
The draws below stay inside these ranges and needn't reach their ends.
Inputs may be any that keep to these rules, and one draw needn't show every extreme that they name: `disc_mask`: in each column of 8 elements the ones form one run of 2 to 4 consecutive rows, counted cyclically in y.
All inputs are finite; a program needn't handle non-finite values.
Results may differ from the reference program's by a relative error of at most 0.0001.
Values sent between devices are 32-bit elements; how exact they have to be, the bound alone decides.
A program may use at most 128 MiB of HBM per device.

```python
import math
import jax
import jax.numpy as jnp
import numpy as np
from jax import lax

ORDER = 8
MODES = 512
E_DEV = 8
ITERS = 2
COLS = 8
ELEMS = 64
NODES = 5184


def draw_disc_mask(key, part):
    key_start, key_length = jax.random.split(key)
    starts = jax.random.randint(key_start, (COLS,), 0, E_DEV)
    lengths = jax.random.randint(key_length, (COLS,), 2, 5)
    column_index = jnp.arange(COLS)
    lengths = jnp.where(column_index == 0, 4, jnp.where(column_index == 1, 2, lengths))
    row_index = jnp.arange(E_DEV)
    marked = (row_index[None, :] - starts[:, None]) % E_DEV < lengths[:, None]
    return marked.astype(jnp.int32).reshape(ELEMS)


def steps_of(rng, shape, shards, low, high):
    loudness, own = 1.0, jax.random.fold_in(rng, 6)
    for position, blocks in shards:
        heights = jnp.exp(jax.random.uniform(jax.random.fold_in(own, position), (blocks,), jnp.float32, low / len(shards), high / len(shards)))
        loudness = loudness * jnp.repeat(heights, shape[position] // blocks).reshape([-1 if axis == position else 1 for axis in range(len(shape))])
    return loudness


def gaussian(own_key, dims, scale, reach, cuts=(), held_as=jnp.bfloat16):
    values = jax.random.normal(own_key, dims, jnp.float32) * scale
    if len(cuts) > 0:
        values = steps_of(own_key, dims, cuts, -0.22, 0.18) * values
    return jnp.clip(values, min=-reach, max=reach).astype(held_as)


def setup_inputs(seed: int = 0) -> dict:
    key_of = jax.random.split(jax.random.key(seed), 5)
    velocity = gaussian(key_of[0], (3, NODES, 2, MODES), 0.5, 3.0, ((1, 8), (3, 4)), jnp.float32)
    column_width = jnp.clip(jnp.exp(math.log(2.0) - 1.3862944 * jax.random.uniform(key_of[1], (COLS,), jnp.float32) ** steps_of(key_of[1], (COLS,), ((0, 8),), -0.2, 0.2)), 0.5, 2.0)
    row_height = jnp.clip(jnp.exp(jax.random.uniform(key_of[2], (E_DEV,), jnp.float32, math.log(0.5), math.log(2.0))), 0.5, 2.0)
    disc_mask = draw_disc_mask(jax.random.fold_in(key_of[4], 71), 0)
    return dict(velocity=velocity, column_width=column_width, row_height=row_height, disc_mask=disc_mask)


gll_points = [-1.0, -0.8997579954114602, -0.6771862795107377, -0.3631174638261782, 0.0, 0.3631174638261782, 0.6771862795107377, 0.8997579954114602, 1.0]
gll_weights = [0.0277777777777778, 0.1654953615608055, 0.2745387125001617, 0.3464285109730463, 0.3715192743764172, 0.3464285109730463, 0.2745387125001617, 0.1654953615608055, 0.0277777777777778]
viscosity = 0.5
time_step = 0.02
thrust_coef = 4.0 / 3.0
highest = lax.Precision.HIGHEST

def node_tables():
    points = np.array(gll_points)
    identity = np.eye(9)
    differences = points[:, None] - points[None, :] + identity
    barycentric = 1.0 / np.prod(differences, axis=1)
    off_diagonal = barycentric[None, :] / barycentric[:, None] / differences * (1.0 - identity)
    derivative = off_diagonal - identity * off_diagonal.sum(axis=1)[:, None]
    return (jnp.asarray(derivative, dtype=jnp.float32), jnp.asarray(np.array(gll_weights), dtype=jnp.float32))

def spectral_tables(mode_count):
    planes = 3 * mode_count
    wave_index = jnp.arange(mode_count, dtype=jnp.int32)
    plane_index = jnp.arange(planes, dtype=jnp.int32)
    phase_index = wave_index[:, None] * plane_index[None, :] % planes
    angles = 2.0 * math.pi / planes * phase_index.astype(jnp.float32)
    cosine_table = jnp.cos(angles)
    sine_table = jnp.sin(angles)
    mode_weight = jnp.where(wave_index == 0, 1.0, 2.0).astype(jnp.float32)[:, None] / math.sqrt(mode_count)
    wave_number = 8.0 / mode_count * wave_index.astype(jnp.float32)[:, None]
    inverse = jnp.concatenate([mode_weight * cosine_table, -mode_weight * sine_table], axis=0)
    spanwise = jnp.concatenate([-wave_number * mode_weight * sine_table, -wave_number * mode_weight * cosine_table], axis=0)
    forward = math.sqrt(mode_count) / planes * jnp.concatenate([cosine_table, -sine_table], axis=0).T
    return (inverse, spanwise, forward)

def assemble(nodal_field):
    upper_layer = nodal_field[:, :, :, 8] + jnp.roll(nodal_field[:, :, :, 0], -1, axis=1)
    nodal_field = jnp.concatenate([jnp.roll(upper_layer, 1, axis=1)[:, :, :, None], nodal_field[:, :, :, 1:8], upper_layer[:, :, :, None]], axis=3)
    upper_layer = nodal_field[:, :, :, :, 8] + jnp.roll(nodal_field[:, :, :, :, 0], -1, axis=2)
    return jnp.concatenate([jnp.roll(upper_layer, 1, axis=2)[:, :, :, :, None], nodal_field[:, :, :, :, 1:8], upper_layer[:, :, :, :, None]], axis=4)

def apply_operator(nodal_field, derivative, quad_weights, ratio_x, ratio_y, jacobian, factor):
    grad_r = jnp.einsum('ij,pcejbl->pceibl', derivative, nodal_field, precision=highest)
    grad_s = jnp.einsum('ij,pceajl->pceail', derivative, nodal_field, precision=highest)
    flux_r = grad_r * quad_weights[None, None, None, :, :, None] * ratio_x[None, :, :, None, None, None]
    flux_s = grad_s * quad_weights[None, None, None, :, :, None] * ratio_y[None, :, :, None, None, None]
    stiffness = jnp.einsum('ji,pcejbl->pceibl', derivative, flux_r, precision=highest) + jnp.einsum('ji,pceajl->pceail', derivative, flux_s, precision=highest)
    masses = jacobian[None, :, :, None, None, None] * quad_weights[None, None, None, :, :, None] * nodal_field
    return assemble(factor * masses + viscosity * stiffness)

def weighted_sum(left_field, right_field, multiplicity):
    return lax.optimization_barrier(jnp.sum(left_field * right_field * multiplicity[None, None, None, :, :, None], axis=(1, 2, 3, 4)))

def reference(velocity, column_width, row_height, disc_mask):
    derivative, weights = node_tables()
    quad_weights = weights[:, None] * weights[None, :]
    node_index = jnp.arange(9)
    edge_count = jnp.where((node_index == 0) | (node_index == 8), 2.0, 1.0).astype(jnp.float32)
    multiplicity = 1.0 / (edge_count[:, None] * edge_count[None, :])
    planes = 3 * MODES
    inverse, spanwise, forward = spectral_tables(MODES)
    nodal_field = velocity.reshape(3, COLS, E_DEV, 9, 9, 2 * MODES)
    wavenumber = 8.0 / MODES * jnp.arange(MODES).astype(jnp.float32)
    plane_index = jnp.arange(planes)
    in_disc = ((plane_index >= 3 * planes // 8) & (plane_index < 5 * planes // 8)).astype(jnp.float32)
    disc_planes = 5 * planes // 8 - 3 * planes // 8
    disc_float = disc_mask.astype(jnp.float32).reshape(COLS, E_DEV)

    def column_tendency(inputs):
        column, col_width, disc_rows = inputs
        values = jnp.einsum('peabl,lq->peabq', column, inverse, precision=highest)
        along_z = jnp.einsum('peabl,lq->peabq', column, spanwise, precision=highest)
        along_x = 2.0 / col_width * jnp.einsum('ij,pejbq->peibq', derivative, values, precision=highest)
        along_y = (2.0 / row_height)[None, :, None, None, None] * jnp.einsum('ij,peajq->peaiq', derivative, values, precision=highest)
        advection = values[0][None] * along_x + values[1][None] * along_y + values[2][None] * along_z
        jacobian = col_width * row_height / 4.0
        node_weight = (disc_rows * jacobian)[:, None, None] * quad_weights[None]
        disc_total = jnp.sum(node_weight[:, :, :, None] * values[0] * values[0] * in_disc)
        disc_area = disc_planes * col_width * jnp.sum(disc_rows * row_height)
        pressure = disc_total / disc_area
        thrust = -(0.5 * thrust_coef * ORDER) * pressure / col_width * disc_rows[:, None, None, None] * in_disc
        tendency = jnp.concatenate([(thrust - advection[0])[None], -advection[1:]], axis=0)
        return jnp.einsum('peabq,ql->peabl', tendency, forward, precision=highest)
    columns = jnp.moveaxis(nodal_field, 1, 0)
    tendencies = lax.map(column_tendency, (columns, column_width, disc_float))
    tendency = jnp.moveaxis(tendencies, 0, 1)
    u_star = nodal_field + time_step * tendency
    jacobian = column_width[:, None] * row_height[None, :] / 4.0
    ratio_x = row_height[None, :] / column_width[:, None]
    ratio_y = column_width[:, None] / row_height[None, :]
    single = 1.0 / time_step + viscosity * wavenumber * wavenumber
    factor = jnp.concatenate([single, single])
    right_side = assemble(jacobian[None, :, :, None, None, None] * quad_weights[None, None, None, :, :, None] * u_star) / time_step
    residual = right_side
    direction = right_side
    solution = jnp.zeros_like(right_side)
    norm_now = weighted_sum(residual, residual, multiplicity)
    for iteration in range(ITERS):
        image_field = apply_operator(direction, derivative, quad_weights, ratio_x, ratio_y, jacobian, factor)
        step_size = (norm_now / weighted_sum(direction, image_field, multiplicity))[:, None, None, None, None, :]
        solution = solution + step_size * direction
        residual = residual - step_size * image_field
        if iteration + 1 < ITERS:
            norm_next = weighted_sum(residual, residual, multiplicity)
            direction = residual + (norm_next / norm_now)[:, None, None, None, None, :] * direction
            norm_now = norm_next
    return solution.reshape(3, NODES, 2, MODES)
```

```python
import math

import jax
import jax.numpy as jnp
import numpy as np
from jax import lax
from jax.experimental import pallas as pl
from jax.experimental.pallas import tpu as pltpu
from jax.sharding import PartitionSpec as P

ORDER = 8
NPT = 9
N2 = 81
PAD = 88

gll_points = [
    -1.0,
    -0.8997579954114602,
    -0.6771862795107377,
    -0.3631174638261782,
    0.0,
    0.3631174638261782,
    0.6771862795107377,
    0.8997579954114602,
    1.0,
]
gll_weights = [
    0.0277777777777778,
    0.1654953615608055,
    0.2745387125001617,
    0.3464285109730463,
    0.3715192743764172,
    0.3464285109730463,
    0.2745387125001617,
    0.1654953615608055,
    0.0277777777777778,
]
viscosity = 0.5
time_step = 0.02
thrust_coef = 4.0 / 3.0
f32 = jnp.float32
bf16 = jnp.bfloat16


def derivative_matrix():
    points = np.array(gll_points)
    identity = np.eye(9)
    differences = points[:, None] - points[None, :] + identity
    barycentric = 1.0 / np.prod(differences, axis=1)
    off_diagonal = barycentric[None, :] / barycentric[:, None] / differences * (1.0 - identity)
    return off_diagonal - identity * off_diagonal.sum(axis=1)[:, None]


def split_host(table):
    import ml_dtypes

    high = table.astype(np.float32).astype(ml_dtypes.bfloat16)
    low = (table - high.astype(np.float64)).astype(np.float32).astype(ml_dtypes.bfloat16)
    return jnp.asarray(high), jnp.asarray(low)


def split(x):
    high = x.astype(bf16)
    return high, (x - high.astype(f32)).astype(bf16)


def dot(a, b):
    return jnp.dot(a, b, preferred_element_type=f32)


def dot_nt(a, b):
    return lax.dot_general(a, b, (((1,), (1,)), ((), ())), preferred_element_type=f32)


def dot3(a, b, d=dot):
    return d(a[0], b[0]) + d(a[0], b[1]) + d(a[1], b[0])


def advect_chunk(groups, modes, tile, planes, scales, x, acc_re, acc_im, small, tabs, scratch):
    ghi, glo, wk, w2 = small
    ch, cl, sh, sl = tabs
    xr, xi, rh, rl, ih, il, col0, press = scratch
    half = planes // 2
    for g in range(groups):
        lanes = slice(g * modes, (g + 1) * modes)
        cw = wk[0:1, lanes]
        ck = wk[1:2, lanes]
        for i in range(3):
            start = (3 * g + i) * 2 * N2
            re = x[pl.ds(start, N2, stride=2), :]
            im = x[pl.ds(start + 1, N2, stride=2), :]
            at = slice(PAD * i, PAD * i + N2)
            zt = slice(3 * PAD + PAD * i, 3 * PAD + PAD * i + N2)
            xr[at, lanes] = cw * re
            xi[at, lanes] = cw * im
            xr[zt, lanes] = -ck * im
            xi[zt, lanes] = ck * re
    full = xr[...]
    rh[...], rl[...] = split(full)
    ih[...], il[...] = split(xi[...])
    col0[...] = jnp.broadcast_to(jnp.sum(full * wk[2:3, :], axis=1, keepdims=True), col0.shape)
    acc_re[...] = jnp.zeros(acc_re.shape, f32)
    acc_im[...] = jnp.zeros(acc_im.shape, f32)
    press[...] = jnp.zeros_like(press)

    def step(q, carry):
        ctab = (ch[q], cl[q])
        stab = (sh[q], sl[q])
        cpart = dot3((rh[...], rl[...]), ctab)
        spart = dot3((ih[...], il[...]), stab)
        lane = lax.broadcasted_iota(jnp.int32, (1, tile), 1) + q * tile
        first = lane == 0
        side_a = cpart - spart
        side_b = jnp.where(first, col0[:, 0:1], cpart + spart)
        plane_b = jnp.where(first, half, planes - lane)
        grad = (ghi[...], glo[...])
        tend = []
        total = jnp.zeros((PAD, tile), f32)
        for side, plane in ((side_a, lane), (side_b, plane_b)):
            inside = ((plane >= 3 * planes // 8) & (plane < 5 * planes // 8)).astype(f32)
            u = [side[PAD * i : PAD * i + PAD] for i in range(3)]
            z = [side[3 * PAD + PAD * i : 4 * PAD + PAD * i] for i in range(3)]
            ux = u[0] * scales[0]
            uy = u[1] * scales[1]
            total = total + u[0] * u[0] * inside
            parts = []
            for i in range(3):
                g = dot3(grad, split(u[i]))
                parts.append(-(ux * g[:PAD] + uy * g[PAD:] + u[2] * z[i]))
            tend.append(jnp.concatenate(parts, axis=0))
        press[...] += total * w2[...]
        plus = split(tend[0] + tend[1])
        minus = split(tend[0] - tend[1])
        acc_re[...] += dot3(plus, ctab, dot_nt)
        acc_im[...] -= dot3(minus, stab, dot_nt)

        @pl.when(q == 0)
        def _():
            acc_re[...] += tend[1][:, 0:1] * (wk[2:3, :] - 1.0)

        return carry

    lax.fori_loop(0, half // tile, step, 0)
    return jnp.sum(jnp.sum(press[...], axis=1, keepdims=True), axis=0, keepdims=True)


def partners(me, groups):
    if groups == 4:
        swap = me + 1 - 2 * lax.rem(me, 2)
        return [swap, lax.rem(me + 2, 4), 3 - me]
    return [lax.rem(me + k, groups) for k in range(1, groups)]


def stiffness_line():
    d = derivative_matrix()
    w = np.array(gll_weights)
    k = d.T @ (w[:, None] * d)
    even = np.zeros((5, 5))
    odd = np.zeros((4, 4))
    for i in range(5):
        for j in range(5):
            even[i, j] = k[i, j] if j == 4 else 0.5 * (k[i, j] + k[i, 8 - j])
    for i in range(4):
        for j in range(4):
            odd[i, j] = 0.5 * (k[i, j] - k[i, 8 - j])
    return even, odd


def line_product(v, even, odd):
    s = [v[j] + v[8 - j] for j in range(4)] + [v[4]]
    t = [v[j] - v[8 - j] for j in range(4)]
    ev = [sum(float(even[i, j]) * s[j] for j in range(5)) for i in range(5)]
    od = [sum(float(odd[i, j]) * t[j] for j in range(4)) for i in range(4)]
    return [ev[i] + od[i] for i in range(4)] + [ev[4]] + [ev[i] - od[i] for i in range(3, -1, -1)]


def window_kernel(
    chunks, groups, elems, modes, peers, tile,
    hx_ref, hy_ref, disc_ref, vel_hbm, tk_hbm, cb_hbm, sb_hbm, rot_hbm, gh_hbm, gl_hbm, wk_hbm, w2_hbm,
    out_hbm,
    vel, tk_ref, cbase, sbase, rot, ghi, glo, wk, w2, ls,
    recv, rs_out, ss_out, acc, faceout, facein, fxs, fxr,
    spec0, ret0, spec1, ret1, ss0, rs0, ss1, rs1,
    pout, pin, pss, psr, pjout, pjin, pjs,
    r, qb, t, vfout, vfin, vfs, rfs, from_left, from_right, qfs, qfr,
    dots, gathered, ds, dr, coef, outv, os,
    ch, cl, sh, sl, mf_ref, rx_ref, ry_ref, jw_ref, cw_ref, th_ref, *scratch,
):
    me = lax.axis_index("elem")
    slot = lax.axis_index("mode")
    planes = 3 * groups * modes
    face = NPT * elems
    w = gll_weights
    even, odd = stiffness_line()
    mult = [0.5] + [1.0] * 7 + [0.5]
    others = partners(slot, groups)
    right, left = lax.rem(me + 1, peers), lax.rem(me + peers - 1, peers)
    last = chunks - 1
    rows0, rows1 = 8 * (NPT - 1), NPT * (NPT - 1)
    mesh_id = pl.DeviceIdType.MESH

    barrier = pltpu.get_barrier_semaphore()
    for other in others:
        pl.semaphore_signal(barrier, inc=1, device_id={"mode": other}, device_id_type=mesh_id)
    for k in range(1, peers):
        pl.semaphore_signal(
            barrier, inc=1, device_id={"elem": lax.rem(me + k, peers)}, device_id_type=mesh_id
        )

    local = [
        pltpu.make_async_copy(source, target, ls.at[n])
        for n, (source, target) in enumerate(
            (
                (cb_hbm, cbase), (sb_hbm, sbase), (rot_hbm, rot), (tk_hbm, tk_ref), (gh_hbm, ghi),
                (gl_hbm, glo), (wk_hbm, wk), (w2_hbm, w2), (vel_hbm, vel),
            )
        )
    ]

    def element(owner, c):
        return vel_hbm.at[:, pl.ds((owner * chunks + c) * N2, N2)]

    own = [
        pltpu.make_async_copy(element(slot, c), recv.at[c, slot], ls.at[len(local) + c])
        for c in range(chunks)
    ]
    for copy in local + own:
        copy.start()

    pl.semaphore_wait(barrier, peers - 1 + groups - 1)

    def remote(source, target, send, receive, **where):
        return pltpu.make_async_remote_copy(
            src_ref=source, dst_ref=target, send_sem=send, recv_sem=receive,
            device_id=where, device_id_type=mesh_id,
        )

    outward = [
        [
            remote(element(other, c), recv.at[c, slot], ss_out.at[c, k], rs_out.at[c, k], mode=other)
            for k, other in enumerate(others)
        ]
        for c in range(chunks)
    ]
    for copies in outward:
        for copy in copies:
            copy.start()

    shape = (elems, modes)
    for e in range(elems):
        mf_ref[e : e + 1, :] = jnp.full((1, modes), hy_ref[e], f32)
        cw_ref[e : e + 1, :] = jnp.full((1, modes), disc_ref[e], jnp.int32).astype(f32)
    hx, hy, disc = jnp.full(shape, hx_ref[0], f32), mf_ref[...], cw_ref[...]
    index = slot * modes + lax.broadcasted_iota(jnp.int32, shape, 1)
    kz = 8.0 / (groups * modes) * index.astype(f32)
    jacobian = hx * hy / 4.0
    disc_planes = 5 * planes // 8 - 3 * planes // 8
    area = disc_planes * hx * jnp.sum(disc * hy, axis=0, keepdims=True)
    mf_ref[...] = jacobian * (1.0 / time_step + viscosity * kz * kz)
    rx_ref[...] = viscosity * hy / hx
    ry_ref[...] = viscosity * hx / hy
    jw_ref[...] = jacobian / time_step
    cw_ref[...] = disc * jacobian
    th_ref[...] = -(0.5 * thrust_coef * ORDER * time_step) / hx * disc / area

    def row(a, b):
        return pl.ds((a * NPT + b) * elems, elems)

    def joined(line):
        top = line[8] + pltpu.roll(line[0], elems - 1, 0)
        return [pltpu.roll(top, 1, 0)] + line[1:8] + [top]

    for copy in local:
        copy.wait()
    xr, xi = scratch[0], scratch[1]
    xr[...] = jnp.zeros_like(xr)
    xi[...] = jnp.zeros_like(xi)
    cos0, sin0 = cbase[...], sbase[...]
    for q in range(planes // 2 // tile):
        cq, sq = rot[:, 2 * q : 2 * q + 1], rot[:, 2 * q + 1 : 2 * q + 2]
        ch[q], cl[q] = split(cos0 * cq - sin0 * sq)
        sh[q], sl[q] = split(sin0 * cq + cos0 * sq)

    mine = vel.reshape(3 * elems * N2 * 2, modes)
    for i in range(3):
        for part in range(2):
            for e in range(elems):
                qb[2 * i + part, pl.ds(e, N2, stride=elems), :] = mine[
                    pl.ds((i * elems + e) * 2 * N2 + part, N2, stride=2), :
                ]

    def masses(p, carry):
        jw = jw_ref[...]
        for a in range(NPT):
            line = joined([qb[p, row(a, b), :] * (jw * (w[a] * w[b])) for b in range(NPT)])
            for b in range(NPT):
                if a == 0:
                    vfout[p, row(0, b), :] = line[b]
                else:
                    r[p, row(a, b), :] = line[b]
                    if b == 8:
                        t[p, row(a, b), :] = jnp.zeros(shape, f32)
        return carry

    lax.fori_loop(0, 6, masses, 0)
    early = remote(vfout, vfin, vfs.at[0], vfs.at[1], elem=left)
    early.start()

    def advance(c):
        for copy in outward[c]:
            copy.wait()
        own[c].wait()
        hy_here = hy_ref[slot * chunks + c]
        scales = (
            2.0 / jnp.full((1, tile), hx_ref[0], f32),
            2.0 / jnp.full((1, tile), hy_here, f32),
        )
        whole = advect_chunk(
            groups, modes, tile, planes, scales, recv.at[c].reshape(groups * 6 * N2, modes),
            acc.at[c, 0], acc.at[c, 1], (ghi, glo, wk, w2), (ch, cl, sh, sl), scratch,
        )
        pout[c : c + 1, :] = jnp.broadcast_to(whole, (1, modes))
        coef_here = math.sqrt(groups * modes) / planes / 4.0
        weight = w2[...] * (coef_here * jnp.full((1, 1), hx_ref[0], f32) * jnp.full((1, 1), hy_here, f32))
        for part in range(2):
            for i in range(3):
                here = slice(PAD * i, PAD * i + PAD)
                acc[c, part, here, :] = acc[c, part, here, :] * weight
                if c > 0:
                    for a in range(NPT):
                        at = PAD * i + NPT * a
                        acc[c, part, at : at + 1, :] += acc[c - 1, part, at + 8 : at + 9, :]
                p = 2 * i + part
                faceout[c, NPT * p : NPT * p + NPT, :] = acc[c, part, PAD * i : PAD * i + NPT, :]
        side = remote(faceout.at[c], facein.at[c], fxs.at[c], fxr.at[c], elem=left)
        side.start()
        return side

    def finish_side(c, side):
        side.wait()
        for part in range(2):
            for i in range(3):
                p = 2 * i + part
                count = NPT if c == last else 8
                at = slice(PAD * i + 8 * NPT, PAD * i + 8 * NPT + count)
                acc[c, part, at, :] += facein[c, NPT * p : NPT * p + count, :]
                for g in range(groups):
                    lanes = slice(g * modes, (g + 1) * modes)
                    if c < last:
                        for a in range(1, NPT):
                            start = PAD * i + NPT * a
                            spec0[c, g, p, 8 * a - 8 : 8 * a, :] = acc[c, part, start : start + 8, lanes]
                    else:
                        spec1[g, p, :, :] = acc[c, part, PAD * i + NPT : PAD * i + N2, lanes]

    returned = []
    for c in range(chunks):
        side = advance(c)
        if c == 0:
            early.wait()
            add = pl.ds(8 * face, face)
            r[:, add, :] = r[:, add, :] + vfin[...]
        if c == last:
            pcopies = [
                remote(pout, pin.at[slot], pss.at[k], psr.at[k], mode=other)
                for k, other in enumerate(others)
            ]
            for copy in pcopies:
                copy.start()
            pin[slot] = pout[...]
        finish_side(c, side)
        if c < last:
            copies = [
                remote(spec0.at[c, other], ret0.at[c, slot], ss0.at[c, k], rs0.at[c, k], mode=other)
                for k, other in enumerate(others)
            ]
            for copy in copies:
                copy.start()
            returned.append(copies)
            ret0[c, slot] = spec0[c, slot]
    pieces = [
        [
            remote(
                spec1.at[other, pl.ds(2 * i, 2)], ret1.at[slot, pl.ds(2 * i, 2)],
                ss1.at[i, k], rs1.at[i, k], mode=other,
            )
            for k, other in enumerate(others)
        ]
        for i in range(3)
    ]
    for copies in pieces:
        for copy in copies:
            copy.start()
    ret1[slot] = spec1[slot]

    for c in range(last):
        for copy in returned[c]:
            copy.wait()
        for g in range(groups):
            e = g * chunks + c
            for p in range(6):
                for a in range(1, NPT):
                    t[p, pl.ds(a * face + e, 8, stride=elems), :] = ret0[c, g, p, 8 * a - 8 : 8 * a, :]
    for copy in pcopies:
        copy.wait()
    pressure = jnp.zeros((1, modes), f32)
    for e in range(elems):
        c = e % chunks
        pressure = pressure + cw_ref[e : e + 1, :] * pin[e // chunks, c : c + 1, :]
    push_here = th_ref[...] * pressure * jw_ref[...]
    pjout[...] = push_here
    push_copy = remote(pjout, pjin, pjs.at[0], pjs.at[1], elem=left)
    push_copy.start()

    def squash(x):
        return jnp.sum(x, axis=0, keepdims=True)

    def add_pieces(i):
        for copy in pieces[i]:
            copy.wait()
        if i == 0:
            push_copy.wait()
        for p in (2 * i, 2 * i + 1):
            for g in range(groups):
                t[p, pl.ds(face + g * chunks + last, rows1, stride=elems), :] = ret1[g, p, :, :]

        def body(p, carry):
            for a in range(1, NPT):
                line = [t[p, row(a, b), :] for b in range(NPT)]
                if i == 0:
                    push = pjout[...] if a < 8 else pjout[...] + pjin[...]
                    push = push * tk_ref[slot, pl.ds(p, 1), :]
                    line = [line[b] + push * (w[a] * w[b]) for b in range(NPT)]
                line = joined(line)
                for b in range(NPT):
                    r[p, row(a, b), :] = r[p, row(a, b), :] + line[b]
            return carry

        lax.fori_loop(2 * i, 2 * i + 2, body, 0)
        copy = remote(
            r.at[pl.ds(2 * i, 2), pl.ds(8 * face, face), :], r.at[pl.ds(2 * i, 2), pl.ds(0, face), :],
            rfs.at[0, i], rfs.at[1, i], elem=right,
        )
        copy.start()
        state[i]["row"] = copy

    def all_dots(n, i):
        return [
            remote(
                dots.at[n, i], gathered.at[n, i, k - 1], ds.at[n, i, k - 1], dr.at[n, i, k - 1],
                elem=lax.rem(me + k, peers),
            )
            for k in range(1, peers)
        ]

    def total_dots(n, i):
        total = dots[n, i]
        for k in range(peers - 1):
            total = total + gathered[n, i, k]
        return total

    def apply_first(i):
        state[i]["row"].wait()
        dots[0, i] = jnp.ones((8, modes), f32)

        def body(p, carry):
            mf, rx, ry = mf_ref[...], rx_ref[...], ry_ref[...]
            for b in range(NPT):
                v = [r[p, row(a, b), :] for a in range(NPT)]
                kx = line_product(v, even, odd)
                rxb = rx * w[b]
                mfb = mf * w[b]
                for a in range(NPT):
                    qb[p, row(a, b), :] = (mfb * w[a]) * v[a] + rxb * kx[a]
            rr = jnp.zeros((elems, modes), f32)
            pq = jnp.zeros((elems, modes), f32)
            for a in range(NPT):
                v = [r[p, row(a, b), :] for b in range(NPT)]
                ky = line_product(v, even, odd)
                rya = ry * w[a]
                line = [qb[p, row(a, b), :] + rya * ky[b] for b in range(NPT)]
                for b in range(NPT):
                    rr = rr + (mult[a] * mult[b]) * (v[b] * v[b])
                    pq = pq + v[b] * line[b]
                line = joined(line)
                for b in range(NPT):
                    qb[p, row(a, b), :] = line[b]
            dots[0, i, pl.ds(p - 2 * i, 1), :] = squash(rr)
            dots[0, i, pl.ds(4 + p - 2 * i, 1), :] = squash(pq)
            return carry

        lax.fori_loop(2 * i, 2 * i + 2, body, 0)
        two = pl.ds(2 * i, 2)
        faces = [
            remote(qb.at[two, pl.ds(8 * face, face), :], from_left.at[i], qfs.at[0, i], qfr.at[0, i], elem=right),
            remote(qb.at[two, pl.ds(0, face), :], from_right.at[i], qfs.at[1, i], qfr.at[1, i], elem=left),
        ]
        sums = all_dots(0, i)
        for copy in faces + sums:
            copy.start()
        state[i]["faces"] = faces
        state[i]["sums"] = sums

    def apply_second(i):
        for copy in state[i]["sums"] + state[i]["faces"]:
            copy.wait()
        total = total_dots(0, i)
        norm = total[0:4]
        alpha = norm / total[4:8]
        state[i]["norm"], state[i]["alpha"] = norm, alpha
        coef[i, 0:4, :] = alpha
        dots[1, i] = jnp.ones((8, modes), f32)
        two = pl.ds(2 * i, 2)
        for at, extra in ((0, from_left), (8 * face, from_right)):
            qb[two, pl.ds(at, face), :] = qb[two, pl.ds(at, face), :] + extra[i]

        def body(p, carry):
            mf, rx, ry = mf_ref[...], rx_ref[...], ry_ref[...]
            al = coef[i, pl.ds(p - 2 * i, 1), :]
            rz = jnp.zeros((elems, modes), f32)
            rr = jnp.zeros((elems, modes), f32)
            for b in range(NPT):
                v = [r[p, row(a, b), :] - al * qb[p, row(a, b), :] for a in range(NPT)]
                kx = line_product(v, even, odd)
                one = jnp.zeros((elems, modes), f32)
                two = jnp.zeros((elems, modes), f32)
                for a in range(NPT):
                    qb[p, row(a, b), :] = v[a]
                    square = v[a] * v[a]
                    one = one + v[a] * kx[a]
                    two = two + w[a] * square
                    rr = rr + (mult[a] * mult[b]) * square
                rz = rz + w[b] * (rx * one + mf * two)
            for a in range(NPT):
                v = [qb[p, row(a, b), :] for b in range(NPT)]
                ky = line_product(v, even, odd)
                one = jnp.zeros((elems, modes), f32)
                for b in range(NPT):
                    one = one + v[b] * ky[b]
                rz = rz + (w[a] * ry) * one
            dots[1, i, pl.ds(p - 2 * i, 1), :] = squash(rr)
            dots[1, i, pl.ds(4 + p - 2 * i, 1), :] = squash(rz)
            return carry

        lax.fori_loop(2 * i, 2 * i + 2, body, 0)
        sums = all_dots(1, i)
        for copy in sums:
            copy.start()
        state[i]["later"] = sums

    def finish(i):
        for copy in state[i]["later"]:
            copy.wait()
        later = total_dots(1, i)
        norm, alpha = state[i]["norm"], state[i]["alpha"]
        following = later[0:4]
        beta = following / norm
        second = following / (later[4:8] - beta * following / alpha)
        first = alpha + second * beta
        for part in range(2):
            p = 2 * i + part
            one, two = first[part : part + 1], second[part : part + 1]
            for e in range(elems):
                at = pl.ds(e, N2, stride=elems)
                outv[i, pl.ds(2 * N2 * e + part, N2, stride=2), :] = one * r[p, at, :] + two * qb[p, at, :]
        copy = pltpu.make_async_copy(outv.at[i], out_hbm.at[i], os.at[i])
        copy.start()
        state[i]["out"] = copy

    state = [{}, {}, {}]
    for stage, i in (
        (add_pieces, 0), (apply_first, 0), (add_pieces, 1), (apply_second, 0), (apply_first, 1), (finish, 0),
        (add_pieces, 2), (apply_second, 1), (apply_first, 2), (finish, 1), (apply_second, 2), (finish, 2),
    ):
        stage(i)
    for i in range(3):
        state[i]["out"].wait()


def window(vel, scalars, tables, groups):
    _, nodes, _, modes = vel.shape
    elems = nodes // N2
    chunks = elems // groups
    count = groups * modes
    half = 3 * count // 2
    tile = tables[1].shape[1]
    peers = lax.axis_size("elem")
    body = lambda *refs: window_kernel(chunks, groups, elems, modes, peers, tile, *refs)
    anywhere = pl.BlockSpec(memory_space=pl.ANY)
    dma = pltpu.SemaphoreType.DMA
    face = NPT * elems
    field = pltpu.VMEM((6, N2 * elems, modes), f32)
    table = pltpu.VMEM((half // tile, count, tile), bf16)
    small = pltpu.VMEM((elems, modes), f32)
    wide = pltpu.VMEM((6 * PAD, count), bf16)
    rows0, rows1 = 8 * (NPT - 1), NPT * (NPT - 1)
    early = max(chunks - 1, 1)
    prow = -(-chunks // 8) * 8
    return pl.pallas_call(
        body,
        out_shape=jax.ShapeDtypeStruct((3, 2 * nodes, modes), f32),
        in_specs=[pl.BlockSpec(memory_space=pltpu.SMEM)] * len(scalars) + [anywhere] * (len(tables) + 1),
        out_specs=anywhere,
        scratch_shapes=[pltpu.VMEM((3, nodes, 2, modes), f32)]
        + [pltpu.VMEM(x.shape, x.dtype) for x in tables]
        + [
            dma((len(tables) + 1 + chunks,)),
            pltpu.VMEM((chunks, groups, 3, N2, 2, modes), f32),
            dma((chunks, groups - 1)),
            dma((chunks, groups - 1)),
            pltpu.VMEM((chunks, 2, 3 * PAD, count), f32),
            pltpu.VMEM((chunks, 6 * NPT, count), f32),
            pltpu.VMEM((chunks, 6 * NPT, count), f32),
            dma((chunks,)),
            dma((chunks,)),
            pltpu.VMEM((early, groups, 6, rows0, modes), f32),
            pltpu.VMEM((early, groups, 6, rows0, modes), f32),
            pltpu.VMEM((groups, 6, rows1, modes), f32),
            pltpu.VMEM((groups, 6, rows1, modes), f32),
            dma((early, groups - 1)),
            dma((early, groups - 1)),
            dma((3, groups - 1)),
            dma((3, groups - 1)),
            pltpu.VMEM((prow, modes), f32),
            pltpu.VMEM((groups, prow, modes), f32),
            dma((groups - 1,)),
            dma((groups - 1,)),
            small,
            small,
            dma((2,)),
            field,
            field,
            field,
            pltpu.VMEM((6, face, modes), f32),
            pltpu.VMEM((6, face, modes), f32),
            dma((2,)),
            dma((2, 3)),
            pltpu.VMEM((3, 2, face, modes), f32),
            pltpu.VMEM((3, 2, face, modes), f32),
            dma((2, 3)),
            dma((2, 3)),
            pltpu.VMEM((2, 3, 8, modes), f32),
            pltpu.VMEM((2, 3, peers - 1, 8, modes), f32),
            dma((2, 3, peers - 1)),
            dma((2, 3, peers - 1)),
            pltpu.VMEM((3, 8, modes), f32),
            pltpu.VMEM((3, 2 * nodes, modes), f32),
            dma((3,)),
            table,
            table,
            table,
            table,
        ]
        + [small] * 6
        + [
            pltpu.VMEM((6 * PAD, count), f32),
            pltpu.VMEM((6 * PAD, count), f32),
            wide,
            wide,
            wide,
            wide,
            pltpu.VMEM((6 * PAD, 128), f32),
            pltpu.VMEM((PAD, tile), f32),
        ],
        compiler_params=pltpu.CompilerParams(
            collective_id=0, has_side_effects=True, vmem_limit_bytes=56 << 20
        ),
    )(*scalars, vel, *tables)


def on_device(velocity, column_width, row_height, disc_mask):
    groups = lax.axis_size("mode")
    _, nodes, _, modes = velocity.shape
    count = groups * modes
    planes = 3 * count
    half = planes // 2
    derivative = derivative_matrix()
    stacked = np.zeros((2 * PAD, PAD))
    stacked[:N2, :N2] = np.kron(derivative, np.eye(9))
    stacked[PAD : PAD + N2, :N2] = np.kron(np.eye(9), derivative)
    grads = split_host(stacked)
    host_k = np.arange(count)
    weight = np.where(host_k == 0, 1.0, 2.0) / math.sqrt(count)
    wk = np.zeros((8, count), np.float32)
    wk[0] = weight
    wk[1] = weight * (8.0 / count) * host_k
    wk[2] = 1.0 - 2.0 * (host_k % 2)
    wk = jnp.asarray(wk)
    w = np.array(gll_weights)
    tile = 256 if half % 256 == 0 else half
    w2 = np.zeros((PAD, 1), np.float32)
    w2[:N2, 0] = (w[:, None] * w[None, :]).reshape(-1)
    w2 = jnp.asarray(w2)

    turn = 2.0 * np.pi / planes
    base = turn * (host_k[:, None] * np.arange(tile)[None, :] % planes)
    steps = turn * (host_k[:, None] * tile * np.arange(half // tile)[None, :] % planes)
    rotation = np.stack([np.cos(steps), np.sin(steps)], axis=2).reshape(count, -1)
    tables = tuple(jnp.asarray(t.astype(np.float32)) for t in (np.cos(base), np.sin(base), rotation))
    tables = tables + grads + (wk, w2)
    in_planes = np.arange(3 * planes // 8, 5 * planes // 8)
    arg = 2.0 * np.pi * ((host_k[:, None] * in_planes[None, :]) % planes) / planes
    profile = math.sqrt(count) / planes * np.stack([np.cos(arg).sum(1), -np.sin(arg).sum(1)])
    profile = np.concatenate([profile, np.zeros((6, count))])
    profile = profile.astype(np.float32).reshape(8, groups, modes).transpose(1, 0, 2)
    tables = (jnp.asarray(profile),) + tables
    result = window(velocity, (column_width, row_height, disc_mask), tables, groups)
    return result.reshape(3, nodes, 2, modes)


def solution(mesh):
    return jax.shard_map(
        on_device,
        mesh=mesh,
        in_specs=(P(None, "elem", None, "mode"), P("elem"), P(), P("elem")),
        out_specs=P(None, "elem", None, "mode"),
        check_vma=False,
    )
```

```python
import math

import jax
import jax.numpy as jnp
import numpy as np
from jax import lax
from jax.experimental import pallas as pl
from jax.experimental.pallas import tpu as pltpu
from jax.sharding import PartitionSpec as P

ORDER = 8
NPT = 9
N2 = 81
PAD = 88

gll_points = [
    -1.0,
    -0.8997579954114602,
    -0.6771862795107377,
    -0.3631174638261782,
    0.0,
    0.3631174638261782,
    0.6771862795107377,
    0.8997579954114602,
    1.0,
]
gll_weights = [
    0.0277777777777778,
    0.1654953615608055,
    0.2745387125001617,
    0.3464285109730463,
    0.3715192743764172,
    0.3464285109730463,
    0.2745387125001617,
    0.1654953615608055,
    0.0277777777777778,
]
viscosity = 0.5
time_step = 0.02
thrust_coef = 4.0 / 3.0
f32 = jnp.float32
bf16 = jnp.bfloat16


def derivative_matrix():
    points = np.array(gll_points)
    identity = np.eye(9)
    differences = points[:, None] - points[None, :] + identity
    barycentric = 1.0 / np.prod(differences, axis=1)
    off_diagonal = barycentric[None, :] / barycentric[:, None] / differences * (1.0 - identity)
    return off_diagonal - identity * off_diagonal.sum(axis=1)[:, None]


def split_host(table):
    import ml_dtypes

    high = table.astype(np.float32).astype(ml_dtypes.bfloat16)
    low = (table - high.astype(np.float64)).astype(np.float32).astype(ml_dtypes.bfloat16)
    return jnp.asarray(high), jnp.asarray(low)


def split(x):
    high = x.astype(bf16)
    return high, (x - high.astype(f32)).astype(bf16)


def dot(a, b):
    return jnp.dot(a, b, preferred_element_type=f32)


def dot_nt(a, b):
    return lax.dot_general(a, b, (((1,), (1,)), ((), ())), preferred_element_type=f32)


def dot3(a, b, d=dot):
    return d(a[0], b[0]) + d(a[0], b[1]) + d(a[1], b[0])


def advect_chunk(groups, modes, tile, planes, scales, x, acc_re, acc_im, small, tabs, scratch):
    ghi, glo, wk, w2 = small
    ch, cl, sh, sl = tabs
    xr, xi, rh, rl, ih, il, col0, press = scratch
    half = planes // 2
    for g in range(groups):
        lanes = slice(g * modes, (g + 1) * modes)
        cw = wk[0:1, lanes]
        ck = wk[1:2, lanes]
        for i in range(3):
            start = (3 * g + i) * 2 * N2
            re = x[pl.ds(start, N2, stride=2), :]
            im = x[pl.ds(start + 1, N2, stride=2), :]
            at = slice(PAD * i, PAD * i + N2)
            zt = slice(3 * PAD + PAD * i, 3 * PAD + PAD * i + N2)
            xr[at, lanes] = cw * re
            xi[at, lanes] = cw * im
            xr[zt, lanes] = -ck * im
            xi[zt, lanes] = ck * re
    full = xr[...]
    rh[...], rl[...] = split(full)
    ih[...], il[...] = split(xi[...])
    col0[...] = jnp.broadcast_to(jnp.sum(full * wk[2:3, :], axis=1, keepdims=True), col0.shape)
    acc_re[...] = jnp.zeros(acc_re.shape, f32)
    acc_im[...] = jnp.zeros(acc_im.shape, f32)
    press[...] = jnp.zeros_like(press)

    def step(q, carry):
        ctab = (ch[q], cl[q])
        stab = (sh[q], sl[q])
        cpart = dot3((rh[...], rl[...]), ctab)
        spart = dot3((ih[...], il[...]), stab)
        lane = lax.broadcasted_iota(jnp.int32, (1, tile), 1) + q * tile
        first = lane == 0
        side_a = cpart - spart
        side_b = jnp.where(first, col0[:, 0:1], cpart + spart)
        plane_b = jnp.where(first, half, planes - lane)
        grad = (ghi[...], glo[...])
        tend = []
        total = jnp.zeros((PAD, tile), f32)
        for side, plane in ((side_a, lane), (side_b, plane_b)):
            inside = ((plane >= 3 * planes // 8) & (plane < 5 * planes // 8)).astype(f32)
            u = [side[PAD * i : PAD * i + PAD] for i in range(3)]
            z = [side[3 * PAD + PAD * i : 4 * PAD + PAD * i] for i in range(3)]
            ux = u[0] * scales[0]
            uy = u[1] * scales[1]
            total = total + u[0] * u[0] * inside
            parts = []
            for i in range(3):
                g = dot3(grad, split(u[i]))
                parts.append(-(ux * g[:PAD] + uy * g[PAD:] + u[2] * z[i]))
            tend.append(jnp.concatenate(parts, axis=0))
        press[...] += total * w2[...]
        plus = split(tend[0] + tend[1])
        minus = split(tend[0] - tend[1])
        acc_re[...] += dot3(plus, ctab, dot_nt)
        acc_im[...] -= dot3(minus, stab, dot_nt)

        @pl.when(q == 0)
        def _():
            acc_re[...] += tend[1][:, 0:1] * (wk[2:3, :] - 1.0)

        return carry

    lax.fori_loop(0, half // tile, step, 0)
    return jnp.sum(jnp.sum(press[...], axis=1, keepdims=True), axis=0, keepdims=True)


def partners(me, groups):
    if groups == 4:
        swap = me + 1 - 2 * lax.rem(me, 2)
        return [3 - me, swap, lax.rem(me + 2, 4)]
    return [lax.rem(me + k, groups) for k in range(1, groups)]


def stiffness_line():
    d = derivative_matrix()
    w = np.array(gll_weights)
    k = d.T @ (w[:, None] * d)
    even = np.zeros((5, 5))
    odd = np.zeros((4, 4))
    for i in range(5):
        for j in range(5):
            even[i, j] = k[i, j] if j == 4 else 0.5 * (k[i, j] + k[i, 8 - j])
    for i in range(4):
        for j in range(4):
            odd[i, j] = 0.5 * (k[i, j] - k[i, 8 - j])
    return even, odd


def line_product(v, even, odd):
    s = [v[j] + v[8 - j] for j in range(4)] + [v[4]]
    t = [v[j] - v[8 - j] for j in range(4)]
    ev = [sum(float(even[i, j]) * s[j] for j in range(5)) for i in range(5)]
    od = [sum(float(odd[i, j]) * t[j] for j in range(4)) for i in range(4)]
    return [ev[i] + od[i] for i in range(4)] + [ev[4]] + [ev[i] - od[i] for i in range(3, -1, -1)]


batches = ((0, 2), (2, 2), (4, 2))
order = "A0 B0 A1 C0 B1 A2 B2 D0 C1 C2 D1 D2"


def window_kernel(
    chunks, groups, elems, modes, peers, tile,
    hx_ref, hy_ref, disc_ref, vel_hbm, tk_hbm, cb_hbm, sb_hbm, rot_hbm, gh_hbm, gl_hbm, wk_hbm, w2_hbm,
    out_hbm,
    vel, tk_ref, cbase, sbase, rot, ghi, glo, wk, w2, ls,
    recv, rs_out, ss_out, acc, faceout, facein, fxs, fxr,
    spec0, ret0, spec1, ret1, specw, retw, ss0, rs0, ss1, rs1, backout, backin, bks,
    pout, pin, pss, psr, pjout, pjin, pjs,
    r, qb, t, vfout, vfin, vfs, rfs, from_left, from_right, qfs, qfr,
    dots, gathered, ds, dr, coef, outv, os,
    ch, cl, sh, sl, mf_ref, rx_ref, ry_ref, jw_ref, cw_ref, th_ref, *scratch,
):
    me = lax.axis_index("elem")
    slot = lax.axis_index("mode")
    planes = 3 * groups * modes
    face = NPT * elems
    w = gll_weights
    even, odd = stiffness_line()
    mult = [0.5] + [1.0] * 7 + [0.5]
    others = partners(slot, groups)
    right, left = lax.rem(me + 1, peers), lax.rem(me + peers - 1, peers)
    last = chunks - 1
    rows1 = NPT * (NPT - 1)
    mesh_id = pl.DeviceIdType.MESH
    final = len(batches) - 1
    wide = batches[final][0]

    barrier = pltpu.get_barrier_semaphore()
    for other in others:
        pl.semaphore_signal(barrier, inc=1, device_id={"mode": other}, device_id_type=mesh_id)
    for k in range(1, peers):
        pl.semaphore_signal(
            barrier, inc=1, device_id={"elem": lax.rem(me + k, peers)}, device_id_type=mesh_id
        )

    local = [
        pltpu.make_async_copy(source, target, ls.at[n])
        for n, (source, target) in enumerate(
            (
                (cb_hbm, cbase), (sb_hbm, sbase), (rot_hbm, rot), (tk_hbm, tk_ref), (gh_hbm, ghi),
                (gl_hbm, glo), (wk_hbm, wk), (w2_hbm, w2), (vel_hbm, vel),
            )
        )
    ]

    def element(owner, c):
        return vel_hbm.at[:, pl.ds((owner * chunks + c) * N2, N2)]

    own = [
        pltpu.make_async_copy(element(slot, c), recv.at[c, slot], ls.at[len(local) + c])
        for c in range(chunks)
    ]
    for copy in local + own:
        copy.start()

    pl.semaphore_wait(barrier, peers - 1 + groups - 1)

    def remote(source, target, send, receive, **where):
        return pltpu.make_async_remote_copy(
            src_ref=source, dst_ref=target, send_sem=send, recv_sem=receive,
            device_id=where, device_id_type=mesh_id,
        )

    outward = [
        [
            remote(element(other, c), recv.at[c, slot], ss_out.at[c, k], rs_out.at[c, k], mode=other)
            for k, other in enumerate(others)
        ]
        for c in range(chunks)
    ]
    for copies in outward:
        for copy in copies:
            copy.start()

    shape = (elems, modes)
    for e in range(elems):
        mf_ref[e : e + 1, :] = jnp.full((1, modes), hy_ref[e], f32)
        cw_ref[e : e + 1, :] = jnp.full((1, modes), disc_ref[e], jnp.int32).astype(f32)
    hx, hy, disc = jnp.full(shape, hx_ref[0], f32), mf_ref[...], cw_ref[...]
    index = slot * modes + lax.broadcasted_iota(jnp.int32, shape, 1)
    kz = 8.0 / (groups * modes) * index.astype(f32)
    jacobian = hx * hy / 4.0
    disc_planes = 5 * planes // 8 - 3 * planes // 8
    area = disc_planes * hx * jnp.sum(disc * hy, axis=0, keepdims=True)
    mf_ref[...] = jacobian * (1.0 / time_step + viscosity * kz * kz)
    rx_ref[...] = viscosity * hy / hx
    ry_ref[...] = viscosity * hx / hy
    jw_ref[...] = jacobian / time_step
    cw_ref[...] = disc * jacobian
    th_ref[...] = -(0.5 * thrust_coef * ORDER * time_step) / hx * disc / area

    def row(a, b):
        return pl.ds((a * NPT + b) * elems, elems)

    def joined(line):
        top = line[8] + pltpu.roll(line[0], elems - 1, 0)
        return [pltpu.roll(top, 1, 0)] + line[1:8] + [top]

    for copy in local:
        copy.wait()
    xr, xi = scratch[0], scratch[1]
    xr[...] = jnp.zeros_like(xr)
    xi[...] = jnp.zeros_like(xi)
    cos0, sin0 = cbase[...], sbase[...]
    for q in range(planes // 2 // tile):
        cq, sq = rot[:, 2 * q : 2 * q + 1], rot[:, 2 * q + 1 : 2 * q + 2]
        ch[q], cl[q] = split(cos0 * cq - sin0 * sq)
        sh[q], sl[q] = split(sin0 * cq + cos0 * sq)

    mine = vel.reshape(3 * elems * N2 * 2, modes)
    for i in range(3):
        for part in range(2):
            for e in range(elems):
                qb[2 * i + part, pl.ds(e, N2, stride=elems), :] = mine[
                    pl.ds((i * elems + e) * 2 * N2 + part, N2, stride=2), :
                ]

    def masses(p, carry):
        jw = jw_ref[...]
        for a in range(NPT):
            line = joined([qb[p, row(a, b), :] * (jw * (w[a] * w[b])) for b in range(NPT)])
            for b in range(NPT):
                if a == 0:
                    vfout[p, row(0, b), :] = line[b]
                else:
                    r[p, row(a, b), :] = line[b]
                    if b == 8:
                        t[p, row(a, b), :] = jnp.zeros(shape, f32)
        return carry

    lax.fori_loop(0, 6, masses, 0)
    early = remote(vfout, vfin, vfs.at[0], vfs.at[1], elem=left)
    early.start()

    def advance(c):
        for copy in outward[c]:
            copy.wait()
        own[c].wait()
        hy_here = hy_ref[slot * chunks + c]
        scales = (
            2.0 / jnp.full((1, tile), hx_ref[0], f32),
            2.0 / jnp.full((1, tile), hy_here, f32),
        )
        whole = advect_chunk(
            groups, modes, tile, planes, scales, recv.at[c].reshape(groups * 6 * N2, modes),
            acc.at[c, 0], acc.at[c, 1], (ghi, glo, wk, w2), (ch, cl, sh, sl), scratch,
        )
        pout[c : c + 1, :] = jnp.broadcast_to(whole, (1, modes))
        coef_here = math.sqrt(groups * modes) / planes / 4.0
        weight = w2[...] * (coef_here * jnp.full((1, 1), hx_ref[0], f32) * jnp.full((1, 1), hy_here, f32))
        for part in range(2):
            for i in range(3):
                here = slice(PAD * i, PAD * i + PAD)
                acc[c, part, here, :] = acc[c, part, here, :] * weight
                if c > 0:
                    for a in range(NPT):
                        at = PAD * i + NPT * a
                        acc[c, part, at : at + 1, :] += acc[c - 1, part, at + 8 : at + 9, :]
                p = 2 * i + part
                faceout[c, NPT * p : NPT * p + NPT, :] = acc[c, part, PAD * i : PAD * i + NPT, :]
                if c == last and p >= wide:
                    at = slice(NPT * (p - wide), NPT * (p - wide) + NPT)
                    backout[at, :] = acc[c, part, PAD * i + 8 * NPT : PAD * i + N2, :]
        sides = [remote(faceout.at[c], facein.at[c], fxs.at[c], fxr.at[c], elem=left)]
        if c == last:
            sides.append(remote(backout, backin, bks.at[0], bks.at[1], elem=right))
        for side in sides:
            side.start()
        return sides

    def finish_side(c, sides):
        for side in sides:
            side.wait()
        for part in range(2):
            for i in range(3):
                p = 2 * i + part
                count = NPT if c == last else 8
                at = slice(PAD * i + 8 * NPT, PAD * i + 8 * NPT + count)
                acc[c, part, at, :] += facein[c, NPT * p : NPT * p + count, :]
                if c == last and p >= wide:
                    at = slice(PAD * i, PAD * i + NPT)
                    acc[c, part, at, :] += backin[NPT * (p - wide) : NPT * (p - wide) + NPT, :]
                for g in range(groups):
                    lanes = slice(g * modes, (g + 1) * modes)
                    if c < last:
                        for a in range(1, NPT):
                            start = PAD * i + NPT * a
                            spec0[c, g, p, 8 * a - 8 : 8 * a, :] = acc[c, part, start : start + 8, lanes]
                    elif p < wide:
                        spec1[g, p, :, :] = acc[c, part, PAD * i + NPT : PAD * i + N2, lanes]
                    else:
                        specw[g, p - wide, :, :] = acc[c, part, PAD * i : PAD * i + N2, lanes]

    returned = []
    for c in range(chunks):
        side = advance(c)
        if c == 0:
            early.wait()
            add = pl.ds(8 * face, face)
            r[:, add, :] = r[:, add, :] + vfin[...]
        if c == last:
            pcopies = [
                remote(pout, pin.at[slot], pss.at[k], psr.at[k], mode=other)
                for k, other in enumerate(others)
            ]
            for copy in pcopies:
                copy.start()
            pin[slot] = pout[...]
        finish_side(c, side)
        if c < last:
            copies = [
                remote(spec0.at[c, other], ret0.at[c, slot], ss0.at[c, k], rs0.at[c, k], mode=other)
                for k, other in enumerate(others)
            ]
            for copy in copies:
                copy.start()
            returned.append(copies)
            ret0[c, slot] = spec0[c, slot]
    pieces = []
    for j, (start, count) in enumerate(batches):
        pieces.append([])
        for k, other in enumerate(others):
            if j < final:
                at = pl.ds(start, count)
                source, target = spec1.at[other, at], ret1.at[slot, at]
            else:
                source, target = specw.at[other], retw.at[slot]
            pieces[j].append(remote(source, target, ss1.at[j, k], rs1.at[j, k], mode=other))
    for copies in pieces:
        for copy in copies:
            copy.start()
    ret1[slot] = spec1[slot]
    retw[slot] = specw[slot]

    for c in range(last):
        for copy in returned[c]:
            copy.wait()
        for g in range(groups):
            e = g * chunks + c
            for p in range(6):
                for a in range(1, NPT):
                    t[p, pl.ds(a * face + e, 8, stride=elems), :] = ret0[c, g, p, 8 * a - 8 : 8 * a, :]
    for copy in pcopies:
        copy.wait()
    pressure = jnp.zeros((1, modes), f32)
    for e in range(elems):
        c = e % chunks
        pressure = pressure + cw_ref[e : e + 1, :] * pin[e // chunks, c : c + 1, :]
    push_here = th_ref[...] * pressure * jw_ref[...]
    pjout[...] = push_here
    push_copy = remote(pjout, pjin, pjs.at[0], pjs.at[1], elem=left)
    push_copy.start()

    def squash(x):
        return jnp.sum(x, axis=0, keepdims=True)

    lately = lax.rem(lax.broadcasted_iota(jnp.int32, shape, 0), chunks) == last

    def send_row(j):
        start, count = batches[j]
        at = pl.ds(start, count)
        state[j]["row"] = remote(
            r.at[at, pl.ds(8 * face, face), :], r.at[at, pl.ds(0, face), :],
            rfs.at[0, j], rfs.at[1, j], elem=right,
        )
        state[j]["row"].start()

    def over(j, body):
        start, count = batches[j]

        def step(p, carry):
            body(p)
            return carry

        lax.fori_loop(start, start + count, step, 0)

    def early_row(j):
        def body(p):
            line = joined([jnp.where(lately, 0.0, t[p, row(8, b), :]) for b in range(NPT)])
            for b in range(NPT):
                r[p, row(8, b), :] = r[p, row(8, b), :] + line[b]

        over(j, body)
        send_row(j)

    def add_pieces(j):
        start, count = batches[j]
        for copy in pieces[j]:
            copy.wait()
        if start == 0:
            push_copy.wait()
        for p in range(start, start + count):
            for g in range(groups):
                e = g * chunks + last
                if j < final:
                    t[p, pl.ds(face + e, rows1, stride=elems), :] = ret1[g, p, :, :]
                else:
                    t[p, pl.ds(e, N2, stride=elems), :] = retw[g, p - wide, :, :]
        if j == final:
            state[j]["row"].wait()

        def body(p):
            for a in range(1 if j < final else 0, NPT):
                line = [t[p, row(a, b), :] for b in range(NPT)]
                if j == final and a in (0, 8):
                    line = [jnp.where(lately, x, 0.0) for x in line]
                if start == 0:
                    push = pjout[...] if a < 8 else pjout[...] + pjin[...]
                    push = push * tk_ref[slot, pl.ds(p, 1), :]
                    line = [line[b] + push * (w[a] * w[b]) for b in range(NPT)]
                line = joined(line)
                for b in range(NPT):
                    r[p, row(a, b), :] = r[p, row(a, b), :] + line[b]

        over(j, body)
        if j < final:
            send_row(j)

    def all_dots(n, i):
        return [
            remote(
                dots.at[n, i], gathered.at[n, i, k - 1], ds.at[n, i, k - 1], dr.at[n, i, k - 1],
                elem=lax.rem(me + k, peers),
            )
            for k in range(1, peers)
        ]

    def total_dots(n, i):
        total = dots[n, i]
        for k in range(peers - 1):
            total = total + gathered[n, i, k]
        return total

    def apply_first(i):
        start, count = batches[i]
        if i < final:
            state[i]["row"].wait()
        dots[0, i] = jnp.ones((4, modes), f32)

        def body(p):
            mf, rx, ry = mf_ref[...], rx_ref[...], ry_ref[...]
            for b in range(NPT):
                v = [r[p, row(a, b), :] for a in range(NPT)]
                kx = line_product(v, even, odd)
                rxb = rx * w[b]
                mfb = mf * w[b]
                for a in range(NPT):
                    qb[p, row(a, b), :] = (mfb * w[a]) * v[a] + rxb * kx[a]
            rr = jnp.zeros((elems, modes), f32)
            pq = jnp.zeros((elems, modes), f32)
            for a in range(NPT):
                v = [r[p, row(a, b), :] for b in range(NPT)]
                ky = line_product(v, even, odd)
                rya = ry * w[a]
                line = [qb[p, row(a, b), :] + rya * ky[b] for b in range(NPT)]
                for b in range(NPT):
                    rr = rr + (mult[a] * mult[b]) * (v[b] * v[b])
                    pq = pq + v[b] * line[b]
                line = joined(line)
                for b in range(NPT):
                    qb[p, row(a, b), :] = line[b]
            dots[0, i, pl.ds(p - start, 1), :] = squash(rr)
            dots[0, i, pl.ds(2 + p - start, 1), :] = squash(pq)

        over(i, body)
        at = pl.ds(start, count)
        faces = [
            remote(
                qb.at[at, pl.ds(8 * face, face), :], from_left.at[at], qfs.at[0, i], qfr.at[0, i],
                elem=right,
            ),
            remote(
                qb.at[at, pl.ds(0, face), :], from_right.at[at], qfs.at[1, i], qfr.at[1, i],
                elem=left,
            ),
        ]
        sums = all_dots(0, i)
        for copy in faces + sums:
            copy.start()
        state[i]["faces"] = faces
        state[i]["sums"] = sums

    def apply_second(i):
        start, count = batches[i]
        for copy in state[i]["sums"] + state[i]["faces"]:
            copy.wait()
        total = total_dots(0, i)
        norm = total[0:2]
        alpha = norm / total[2:4]
        state[i]["norm"], state[i]["alpha"] = norm, alpha
        coef[i, 0:2, :] = alpha
        dots[1, i] = jnp.ones((4, modes), f32)
        here = pl.ds(start, count)
        for at, extra in ((0, from_left), (8 * face, from_right)):
            qb[here, pl.ds(at, face), :] = qb[here, pl.ds(at, face), :] + extra[here]

        def body(p):
            mf, rx, ry = mf_ref[...], rx_ref[...], ry_ref[...]
            al = coef[i, pl.ds(p - start, 1), :]
            rz = jnp.zeros((elems, modes), f32)
            rr = jnp.zeros((elems, modes), f32)
            for b in range(NPT):
                v = [r[p, row(a, b), :] - al * qb[p, row(a, b), :] for a in range(NPT)]
                kx = line_product(v, even, odd)
                one = jnp.zeros((elems, modes), f32)
                two = jnp.zeros((elems, modes), f32)
                for a in range(NPT):
                    qb[p, row(a, b), :] = v[a]
                    square = v[a] * v[a]
                    one = one + v[a] * kx[a]
                    two = two + w[a] * square
                    rr = rr + (mult[a] * mult[b]) * square
                rz = rz + w[b] * (rx * one + mf * two)
            for a in range(NPT):
                v = [qb[p, row(a, b), :] for b in range(NPT)]
                ky = line_product(v, even, odd)
                one = jnp.zeros((elems, modes), f32)
                for b in range(NPT):
                    one = one + v[b] * ky[b]
                rz = rz + (w[a] * ry) * one
            dots[1, i, pl.ds(p - start, 1), :] = squash(rr)
            dots[1, i, pl.ds(2 + p - start, 1), :] = squash(rz)

        over(i, body)
        sums = all_dots(1, i)
        for copy in sums:
            copy.start()
        state[i]["later"] = sums

    def finish(i):
        for copy in state[i]["later"]:
            copy.wait()
        later = total_dots(1, i)
        norm, alpha = state[i]["norm"], state[i]["alpha"]
        following = later[0:2]
        beta = following / norm
        second = following / (later[2:4] - beta * following / alpha)
        first = alpha + second * beta
        start, count = batches[i]
        for p in range(start, start + count):
            n = p - start
            one, two = first[n : n + 1], second[n : n + 1]
            for e in range(elems):
                at = pl.ds(e, N2, stride=elems)
                outv[p // 2, pl.ds(2 * N2 * e + p % 2, N2, stride=2), :] = (
                    one * r[p, at, :] + two * qb[p, at, :]
                )
            ready.append(p)
            if p ^ 1 in ready:
                copy = pltpu.make_async_copy(outv.at[p // 2], out_hbm.at[p // 2], os.at[p // 2])
                copy.start()
                outgoing.append(copy)

    ready, outgoing = [], []
    state = [{} for _ in batches]
    early_row(final)
    stages = {"A": add_pieces, "B": apply_first, "C": apply_second, "D": finish}
    for name in order.split():
        stages[name[0]](int(name[1:]))
    for copy in outgoing:
        copy.wait()


def deliver(source, target, sem):
    copy = pltpu.make_async_copy(source, target, sem)
    copy.start()
    copy.wait()


def window(vel, scalars, tables, groups):
    _, nodes, _, modes = vel.shape
    elems = nodes // N2
    chunks = elems // groups
    count = groups * modes
    half = 3 * count // 2
    tile = tables[1].shape[1]
    peers = lax.axis_size("elem")
    body = lambda *refs: window_kernel(chunks, groups, elems, modes, peers, tile, *refs)
    anywhere = pl.BlockSpec(memory_space=pl.ANY)
    dma = pltpu.SemaphoreType.DMA
    face = NPT * elems
    field = pltpu.VMEM((6, N2 * elems, modes), f32)
    table = pltpu.VMEM((half // tile, count, tile), bf16)
    small = pltpu.VMEM((elems, modes), f32)
    wide = pltpu.VMEM((6 * PAD, count), bf16)
    rows0, rows1 = 8 * (NPT - 1), NPT * (NPT - 1)
    parts = len(batches)
    wide_count = batches[-1][1]
    early = max(chunks - 1, 1)
    prow = -(-chunks // 8) * 8
    result = pl.pallas_call(
        body,
        out_shape=jax.ShapeDtypeStruct((3, 2 * nodes, modes), f32),
        in_specs=[pl.BlockSpec(memory_space=pltpu.SMEM)] * len(scalars)
        + [pl.BlockSpec(memory_space=pltpu.HBM)] * (len(tables) + 1),
        out_specs=anywhere,
        scratch_shapes=[pltpu.VMEM((3, nodes, 2, modes), f32)]
        + [pltpu.VMEM(x.shape, x.dtype) for x in tables]
        + [
            dma((len(tables) + 1 + chunks,)),
            pltpu.VMEM((chunks, groups, 3, N2, 2, modes), f32),
            dma((chunks, groups - 1)),
            dma((chunks, groups - 1)),
            pltpu.VMEM((chunks, 2, 3 * PAD, count), f32),
            pltpu.VMEM((chunks, 6 * NPT, count), f32),
            pltpu.VMEM((chunks, 6 * NPT, count), f32),
            dma((chunks,)),
            dma((chunks,)),
            pltpu.VMEM((early, groups, 6, rows0, modes), f32),
            pltpu.VMEM((early, groups, 6, rows0, modes), f32),
            pltpu.VMEM((groups, 6 - wide_count, rows1, modes), f32),
            pltpu.VMEM((groups, 6 - wide_count, rows1, modes), f32),
            pltpu.VMEM((groups, wide_count, N2, modes), f32),
            pltpu.VMEM((groups, wide_count, N2, modes), f32),
            dma((early, groups - 1)),
            dma((early, groups - 1)),
            dma((parts, groups - 1)),
            dma((parts, groups - 1)),
            pltpu.VMEM((wide_count * NPT, count), f32),
            pltpu.VMEM((wide_count * NPT, count), f32),
            dma((2,)),
            pltpu.VMEM((prow, modes), f32),
            pltpu.VMEM((groups, prow, modes), f32),
            dma((groups - 1,)),
            dma((groups - 1,)),
            small,
            small,
            dma((2,)),
            field,
            field,
            field,
            pltpu.VMEM((6, face, modes), f32),
            pltpu.VMEM((6, face, modes), f32),
            dma((2,)),
            dma((2, parts)),
            pltpu.VMEM((6, face, modes), f32),
            pltpu.VMEM((6, face, modes), f32),
            dma((2, parts)),
            dma((2, parts)),
            pltpu.VMEM((2, parts, 4, modes), f32),
            pltpu.VMEM((2, parts, peers - 1, 4, modes), f32),
            dma((2, parts, peers - 1)),
            dma((2, parts, peers - 1)),
            pltpu.VMEM((parts, 2, modes), f32),
            pltpu.VMEM((3, 2 * nodes, modes), f32),
            dma((3,)),
            table,
            table,
            table,
            table,
        ]
        + [small] * 6
        + [
            pltpu.VMEM((6 * PAD, count), f32),
            pltpu.VMEM((6 * PAD, count), f32),
            wide,
            wide,
            wide,
            wide,
            pltpu.VMEM((6 * PAD, 128), f32),
            pltpu.VMEM((PAD, tile), f32),
        ],
        compiler_params=pltpu.CompilerParams(
            collective_id=0, has_side_effects=True, vmem_limit_bytes=40 << 20
        ),
    )(scalars[0], *[pltpu.with_memory_space_constraint(x, pltpu.HBM) for x in (*scalars[1:], vel, *tables)])
    return pl.pallas_call(
        deliver,
        out_shape=jax.ShapeDtypeStruct((3, 2 * nodes, modes), f32),
        in_specs=[anywhere],
        out_specs=pl.BlockSpec(memory_space=pltpu.HBM),
        scratch_shapes=[dma],
        compiler_params=pltpu.CompilerParams(vmem_limit_bytes=1 << 20),
    )(result)


def on_device(velocity, column_width, row_height, disc_mask):
    groups = lax.axis_size("mode")
    _, nodes, _, modes = velocity.shape
    count = groups * modes
    planes = 3 * count
    half = planes // 2
    derivative = derivative_matrix()
    stacked = np.zeros((2 * PAD, PAD))
    stacked[:N2, :N2] = np.kron(derivative, np.eye(9))
    stacked[PAD : PAD + N2, :N2] = np.kron(np.eye(9), derivative)
    grads = split_host(stacked)
    host_k = np.arange(count)
    weight = np.where(host_k == 0, 1.0, 2.0) / math.sqrt(count)
    wk = np.zeros((8, count), np.float32)
    wk[0] = weight
    wk[1] = weight * (8.0 / count) * host_k
    wk[2] = 1.0 - 2.0 * (host_k % 2)
    wk = jnp.asarray(wk)
    w = np.array(gll_weights)
    tile = 256 if half % 256 == 0 else half
    w2 = np.zeros((PAD, 1), np.float32)
    w2[:N2, 0] = (w[:, None] * w[None, :]).reshape(-1)
    w2 = jnp.asarray(w2)

    turn = 2.0 * np.pi / planes
    base = turn * (host_k[:, None] * np.arange(tile)[None, :] % planes)
    steps = turn * (host_k[:, None] * tile * np.arange(half // tile)[None, :] % planes)
    rotation = np.stack([np.cos(steps), np.sin(steps)], axis=2).reshape(count, -1)
    tables = tuple(jnp.asarray(t.astype(np.float32)) for t in (np.cos(base), np.sin(base), rotation))
    tables = tables + grads + (wk, w2)
    in_planes = np.arange(3 * planes // 8, 5 * planes // 8)
    arg = 2.0 * np.pi * ((host_k[:, None] * in_planes[None, :]) % planes) / planes
    profile = math.sqrt(count) / planes * np.stack([np.cos(arg).sum(1), -np.sin(arg).sum(1)])
    profile = np.concatenate([profile, np.zeros((6, count))])
    profile = profile.astype(np.float32).reshape(8, groups, modes).transpose(1, 0, 2)
    tables = (jnp.asarray(profile),) + tables
    result = window(velocity, (column_width, row_height, disc_mask), tables, groups)
    return result.reshape(3, nodes, 2, modes)


def solution(mesh):
    return jax.shard_map(
        on_device,
        mesh=mesh,
        in_specs=(P(None, "elem", None, "mode"), P("elem"), P(), P("elem")),
        out_specs=P(None, "elem", None, "mode"),
        check_vma=False,
    )
```

```python
import math

import jax
import jax.numpy as jnp
import numpy as np
from jax import lax
from jax.experimental import pallas as pl
from jax.experimental.pallas import tpu as pltpu
from jax.sharding import PartitionSpec as P

ORDER = 8
NPT = 9
N2 = 81
PAD = 88

gll_points = [
    -1.0,
    -0.8997579954114602,
    -0.6771862795107377,
    -0.3631174638261782,
    0.0,
    0.3631174638261782,
    0.6771862795107377,
    0.8997579954114602,
    1.0,
]
gll_weights = [
    0.0277777777777778,
    0.1654953615608055,
    0.2745387125001617,
    0.3464285109730463,
    0.3715192743764172,
    0.3464285109730463,
    0.2745387125001617,
    0.1654953615608055,
    0.0277777777777778,
]
viscosity = 0.5
time_step = 0.02
thrust_coef = 4.0 / 3.0
f32 = jnp.float32
bf16 = jnp.bfloat16


def derivative_matrix():
    points = np.array(gll_points)
    identity = np.eye(9)
    differences = points[:, None] - points[None, :] + identity
    barycentric = 1.0 / np.prod(differences, axis=1)
    off_diagonal = barycentric[None, :] / barycentric[:, None] / differences * (1.0 - identity)
    return off_diagonal - identity * off_diagonal.sum(axis=1)[:, None]


def split_host(table):
    import ml_dtypes

    high = table.astype(np.float32).astype(ml_dtypes.bfloat16)
    low = (table - high.astype(np.float64)).astype(np.float32).astype(ml_dtypes.bfloat16)
    return jnp.asarray(high), jnp.asarray(low)


def split(x):
    high = x.astype(bf16)
    return high, (x - high.astype(f32)).astype(bf16)


def dot(a, b):
    return jnp.dot(a, b, preferred_element_type=f32)


def dot_nt(a, b):
    return lax.dot_general(a, b, (((1,), (1,)), ((), ())), preferred_element_type=f32)


def dot3(a, b, d=dot):
    return d(a[0], b[0]) + d(a[0], b[1]) + d(a[1], b[0])


def advect_chunk(groups, modes, tile, planes, scales, x, acc_re, acc_im, small, tabs, scratch):
    ghi, glo, wk, w2 = small
    ch, cl, sh, sl = tabs
    xr, xi, rh, rl, ih, il, col0, press = scratch
    half = planes // 2
    for g in range(groups):
        lanes = slice(g * modes, (g + 1) * modes)
        cw = wk[0:1, lanes]
        ck = wk[1:2, lanes]
        for i in range(3):
            start = (3 * g + i) * 2 * N2
            re = x[pl.ds(start, N2, stride=2), :]
            im = x[pl.ds(start + 1, N2, stride=2), :]
            at = slice(PAD * i, PAD * i + N2)
            zt = slice(3 * PAD + PAD * i, 3 * PAD + PAD * i + N2)
            xr[at, lanes] = cw * re
            xi[at, lanes] = cw * im
            xr[zt, lanes] = -ck * im
            xi[zt, lanes] = ck * re
    full = xr[...]
    rh[...], rl[...] = split(full)
    ih[...], il[...] = split(xi[...])
    col0[...] = jnp.broadcast_to(jnp.sum(full * wk[2:3, :], axis=1, keepdims=True), col0.shape)
    acc_re[...] = jnp.zeros(acc_re.shape, f32)
    acc_im[...] = jnp.zeros(acc_im.shape, f32)
    press[...] = jnp.zeros_like(press)

    def step(q, carry):
        ctab = (ch[q], cl[q])
        stab = (sh[q], sl[q])
        cpart = dot3((rh[...], rl[...]), ctab)
        spart = dot3((ih[...], il[...]), stab)
        lane = lax.broadcasted_iota(jnp.int32, (1, tile), 1) + q * tile
        first = lane == 0
        side_a = cpart - spart
        side_b = jnp.where(first, col0[:, 0:1], cpart + spart)
        plane_b = jnp.where(first, half, planes - lane)
        grad = (ghi[...], glo[...])
        tend = []
        total = jnp.zeros((PAD, tile), f32)
        for side, plane in ((side_a, lane), (side_b, plane_b)):
            inside = ((plane >= 3 * planes // 8) & (plane < 5 * planes // 8)).astype(f32)
            u = [side[PAD * i : PAD * i + PAD] for i in range(3)]
            z = [side[3 * PAD + PAD * i : 4 * PAD + PAD * i] for i in range(3)]
            ux = u[0] * scales[0]
            uy = u[1] * scales[1]
            total = total + u[0] * u[0] * inside
            parts = []
            for i in range(3):
                g = dot3(grad, split(u[i]))
                parts.append(-(ux * g[:PAD] + uy * g[PAD:] + u[2] * z[i]))
            tend.append(jnp.concatenate(parts, axis=0))
        press[...] += total * w2[...]
        plus = split(tend[0] + tend[1])
        minus = split(tend[0] - tend[1])
        acc_re[...] += dot3(plus, ctab, dot_nt)
        acc_im[...] -= dot3(minus, stab, dot_nt)

        @pl.when(q == 0)
        def _():
            acc_re[...] += tend[1][:, 0:1] * (wk[2:3, :] - 1.0)

        return carry

    lax.fori_loop(0, half // tile, step, 0)
    return jnp.sum(jnp.sum(press[...], axis=1, keepdims=True), axis=0, keepdims=True)


def partners(me, groups):
    if groups == 4:
        swap = me + 1 - 2 * lax.rem(me, 2)
        return [3 - me, swap, lax.rem(me + 2, 4)]
    return [lax.rem(me + k, groups) for k in range(1, groups)]


def stiffness_line():
    d = derivative_matrix()
    w = np.array(gll_weights)
    k = d.T @ (w[:, None] * d)
    even = np.zeros((5, 5))
    odd = np.zeros((4, 4))
    for i in range(5):
        for j in range(5):
            even[i, j] = k[i, j] if j == 4 else 0.5 * (k[i, j] + k[i, 8 - j])
    for i in range(4):
        for j in range(4):
            odd[i, j] = 0.5 * (k[i, j] - k[i, 8 - j])
    return even, odd


def line_product(v, even, odd):
    s = [v[j] + v[8 - j] for j in range(4)] + [v[4]]
    t = [v[j] - v[8 - j] for j in range(4)]
    ev = [sum(float(even[i, j]) * s[j] for j in range(5)) for i in range(5)]
    od = [sum(float(odd[i, j]) * t[j] for j in range(4)) for i in range(4)]
    return [ev[i] + od[i] for i in range(4)] + [ev[4]] + [ev[i] - od[i] for i in range(3, -1, -1)]


batches = ((0, 2), (2, 2), (4, 2))
order = "A0B0A1C0B1A2B2D0C1C2D1D2"
out_edge, out_inner = "r0s0t0r1s1t1", "r0s0t0r1s1t1"
early_edge, early_inner = "rst", "rst"
late_edge, late_inner = "r0s0t0r1s1t1r2s2t2", "t0s0r0t1s1r1t2s2r2"


def window_kernel(
    chunks, groups, elems, modes, peers, tile,
    hx_hbm, hy_hbm, disc_hbm, vel_hbm, tk_hbm, cb_hbm, sb_hbm, rot_hbm, gh_hbm, gl_hbm, wk_hbm, w2_hbm,
    out_hbm,
    hx_ref, hy_ref, disc_ref, vel, tk_ref, cbase, sbase, rot, ghi, glo, wk, w2, ls,
    recv, rs_out, ss_out, acc, faceout, facein, fxs, fxr,
    spec0, ret0, spec1, ret1, specw, retw, ss0, rs0, ss1, rs1, backout, backin, bks,
    pout, pin, pss, psr, pjout, pjin, pjs,
    r, qb, t, vfout, vfin, vfs, rfs, from_left, from_right, qfs, qfr,
    dots, gathered, ds, dr, coef, outv, os,
    ch, cl, sh, sl, mf_ref, rx_ref, ry_ref, jw_ref, cw_ref, th_ref, *scratch,
):
    me = lax.axis_index("elem")
    slot = lax.axis_index("mode")
    planes = 3 * groups * modes
    face = NPT * elems
    w = gll_weights
    even, odd = stiffness_line()
    mult = [0.5] + [1.0] * 7 + [0.5]
    others = partners(slot, groups)
    right, left = lax.rem(me + 1, peers), lax.rem(me + peers - 1, peers)
    last = chunks - 1
    rows1 = NPT * (NPT - 1)
    mesh_id = pl.DeviceIdType.MESH
    final = len(batches) - 1
    wide = batches[final][0]

    barrier = pltpu.get_barrier_semaphore()
    for other in others:
        pl.semaphore_signal(barrier, inc=1, device_id={"mode": other}, device_id_type=mesh_id)
    for k in range(1, peers):
        pl.semaphore_signal(
            barrier, inc=1, device_id={"elem": lax.rem(me + k, peers)}, device_id_type=mesh_id
        )

    local = [
        pltpu.make_async_copy(source, target, ls.at[n])
        for n, (source, target) in enumerate(
            (
                (cb_hbm, cbase), (sb_hbm, sbase), (rot_hbm, rot), (tk_hbm, tk_ref), (gh_hbm, ghi),
                (gl_hbm, glo), (wk_hbm, wk), (w2_hbm, w2), (vel_hbm, vel),
                (hx_hbm, hx_ref), (hy_hbm, hy_ref), (disc_hbm, disc_ref),
            )
        )
    ]

    def element(owner, c):
        return vel_hbm.at[:, pl.ds((owner * chunks + c) * N2, N2)]

    own = [
        pltpu.make_async_copy(element(slot, c), recv.at[c, slot], ls.at[len(local) + c])
        for c in range(chunks)
    ]
    for copy in local + own:
        copy.start()

    pl.semaphore_wait(barrier, peers - 1 + groups - 1)

    def remote(source, target, send, receive, **where):
        return pltpu.make_async_remote_copy(
            src_ref=source, dst_ref=target, send_sem=send, recv_sem=receive,
            device_id=where, device_id_type=mesh_id,
        )

    outward = [
        [
            remote(element(other, c), recv.at[c, slot], ss_out.at[c, k], rs_out.at[c, k], mode=other)
            for k, other in enumerate(others)
        ]
        for c in range(chunks)
    ]
    edge = (slot == 0) | (slot == groups - 1)

    def launch(copies, edge_order, inner_order):
        if groups != 4 or len(edge_order) != 6 * len(copies):
            for some in copies:
                for copy in some:
                    copy.start()
            return
        for here, text in ((edge, edge_order), (jnp.logical_not(edge), inner_order)):

            @pl.when(here)
            def _():
                for k, j in zip(text[::2], text[1::2]):
                    copies[int(j)]["rst".index(k)].start()

    launch(outward, out_edge, out_inner)

    shape = (elems, modes)
    for copy in local:
        copy.wait()
    for e in range(elems):
        mf_ref[e : e + 1, :] = jnp.full((1, modes), hy_ref[e], f32)
        cw_ref[e : e + 1, :] = jnp.full((1, modes), disc_ref[e], jnp.int32).astype(f32)
    hx, hy, disc = jnp.full(shape, hx_ref[0], f32), mf_ref[...], cw_ref[...]
    index = slot * modes + lax.broadcasted_iota(jnp.int32, shape, 1)
    kz = 8.0 / (groups * modes) * index.astype(f32)
    jacobian = hx * hy / 4.0
    disc_planes = 5 * planes // 8 - 3 * planes // 8
    area = disc_planes * hx * jnp.sum(disc * hy, axis=0, keepdims=True)
    mf_ref[...] = jacobian * (1.0 / time_step + viscosity * kz * kz)
    rx_ref[...] = viscosity * hy / hx
    ry_ref[...] = viscosity * hx / hy
    jw_ref[...] = jacobian / time_step
    cw_ref[...] = disc * jacobian
    th_ref[...] = -(0.5 * thrust_coef * ORDER * time_step) / hx * disc / area

    def row(a, b):
        return pl.ds((a * NPT + b) * elems, elems)

    def joined(line):
        top = line[8] + pltpu.roll(line[0], elems - 1, 0)
        return [pltpu.roll(top, 1, 0)] + line[1:8] + [top]

    xr, xi = scratch[0], scratch[1]
    xr[...] = jnp.zeros_like(xr)
    xi[...] = jnp.zeros_like(xi)
    cos0, sin0 = cbase[...], sbase[...]
    for q in range(planes // 2 // tile):
        cq, sq = rot[:, 2 * q : 2 * q + 1], rot[:, 2 * q + 1 : 2 * q + 2]
        ch[q], cl[q] = split(cos0 * cq - sin0 * sq)
        sh[q], sl[q] = split(sin0 * cq + cos0 * sq)

    mine = vel.reshape(3 * elems * N2 * 2, modes)
    for i in range(3):
        for part in range(2):
            for e in range(elems):
                qb[2 * i + part, pl.ds(e, N2, stride=elems), :] = mine[
                    pl.ds((i * elems + e) * 2 * N2 + part, N2, stride=2), :
                ]

    def masses(p, carry):
        jw = jw_ref[...]
        for a in range(NPT):
            line = joined([qb[p, row(a, b), :] * (jw * (w[a] * w[b])) for b in range(NPT)])
            for b in range(NPT):
                if a == 0:
                    vfout[p, row(0, b), :] = line[b]
                else:
                    r[p, row(a, b), :] = line[b]
                    if b == 8:
                        t[p, row(a, b), :] = jnp.zeros(shape, f32)
        return carry

    lax.fori_loop(0, 6, masses, 0)
    early = remote(vfout, vfin, vfs.at[0], vfs.at[1], elem=left)
    early.start()

    def advance(c):
        for copy in outward[c]:
            copy.wait()
        own[c].wait()
        hy_here = hy_ref[slot * chunks + c]
        scales = (
            2.0 / jnp.full((1, tile), hx_ref[0], f32),
            2.0 / jnp.full((1, tile), hy_here, f32),
        )
        whole = advect_chunk(
            groups, modes, tile, planes, scales, recv.at[c].reshape(groups * 6 * N2, modes),
            acc.at[c, 0], acc.at[c, 1], (ghi, glo, wk, w2), (ch, cl, sh, sl), scratch,
        )
        pout[c : c + 1, :] = jnp.broadcast_to(whole, (1, modes))
        coef_here = math.sqrt(groups * modes) / planes / 4.0
        weight = w2[...] * (coef_here * jnp.full((1, 1), hx_ref[0], f32) * jnp.full((1, 1), hy_here, f32))
        for part in range(2):
            for i in range(3):
                here = slice(PAD * i, PAD * i + PAD)
                acc[c, part, here, :] = acc[c, part, here, :] * weight
                if c > 0:
                    for a in range(NPT):
                        at = PAD * i + NPT * a
                        acc[c, part, at : at + 1, :] += acc[c - 1, part, at + 8 : at + 9, :]
                p = 2 * i + part
                faceout[c, NPT * p : NPT * p + NPT, :] = acc[c, part, PAD * i : PAD * i + NPT, :]
                if c == last and p >= wide:
                    at = slice(NPT * (p - wide), NPT * (p - wide) + NPT)
                    backout[at, :] = acc[c, part, PAD * i + 8 * NPT : PAD * i + N2, :]
        sides = [remote(faceout.at[c], facein.at[c], fxs.at[c], fxr.at[c], elem=left)]
        if c == last:
            sides.append(remote(backout, backin, bks.at[0], bks.at[1], elem=right))
        for side in sides:
            side.start()
        return sides

    def finish_side(c, sides):
        for side in sides:
            side.wait()
        for part in range(2):
            for i in range(3):
                p = 2 * i + part
                count = NPT if c == last else 8
                at = slice(PAD * i + 8 * NPT, PAD * i + 8 * NPT + count)
                acc[c, part, at, :] += facein[c, NPT * p : NPT * p + count, :]
                if c == last and p >= wide:
                    at = slice(PAD * i, PAD * i + NPT)
                    acc[c, part, at, :] += backin[NPT * (p - wide) : NPT * (p - wide) + NPT, :]
                for g in range(groups):
                    lanes = slice(g * modes, (g + 1) * modes)
                    if c < last:
                        for a in range(1, NPT):
                            start = PAD * i + NPT * a
                            spec0[c, g, p, 8 * a - 8 : 8 * a, :] = acc[c, part, start : start + 8, lanes]
                    elif p < wide:
                        spec1[g, p, :, :] = acc[c, part, PAD * i + NPT : PAD * i + N2, lanes]
                    else:
                        specw[g, p - wide, :, :] = acc[c, part, PAD * i : PAD * i + N2, lanes]

    returned = []
    for c in range(chunks):
        side = advance(c)
        if c == 0:
            early.wait()
            add = pl.ds(8 * face, face)
            r[:, add, :] = r[:, add, :] + vfin[...]
        if c == last:
            pcopies = [
                remote(pout, pin.at[slot], pss.at[k], psr.at[k], mode=other)
                for k, other in enumerate(others)
            ]
            for copy in pcopies:
                copy.start()
            pin[slot] = pout[...]
        finish_side(c, side)
        if c < last:
            copies = [
                remote(spec0.at[c, other], ret0.at[c, slot], ss0.at[c, k], rs0.at[c, k], mode=other)
                for k, other in enumerate(others)
            ]
            launch([copies], early_edge[0] + "0" + early_edge[1] + "0" + early_edge[2] + "0",
                   early_inner[0] + "0" + early_inner[1] + "0" + early_inner[2] + "0")
            returned.append(copies)
            ret0[c, slot] = spec0[c, slot]
    pieces = []
    for j, (start, count) in enumerate(batches):
        pieces.append([])
        for k, other in enumerate(others):
            if j < final:
                at = pl.ds(start, count)
                source, target = spec1.at[other, at], ret1.at[slot, at]
            else:
                source, target = specw.at[other], retw.at[slot]
            pieces[j].append(remote(source, target, ss1.at[j, k], rs1.at[j, k], mode=other))
    launch(pieces, late_edge, late_inner)
    ret1[slot] = spec1[slot]
    retw[slot] = specw[slot]

    for c in range(last):
        for copy in returned[c]:
            copy.wait()
        for g in range(groups):
            e = g * chunks + c
            for p in range(6):
                for a in range(1, NPT):
                    t[p, pl.ds(a * face + e, 8, stride=elems), :] = ret0[c, g, p, 8 * a - 8 : 8 * a, :]
    for copy in pcopies:
        copy.wait()
    pressure = jnp.zeros((1, modes), f32)
    for e in range(elems):
        c = e % chunks
        pressure = pressure + cw_ref[e : e + 1, :] * pin[e // chunks, c : c + 1, :]
    push_here = th_ref[...] * pressure * jw_ref[...]
    pjout[...] = push_here
    push_copy = remote(pjout, pjin, pjs.at[0], pjs.at[1], elem=left)
    push_copy.start()

    def squash(x):
        return jnp.sum(x, axis=0, keepdims=True)

    lately = lax.rem(lax.broadcasted_iota(jnp.int32, shape, 0), chunks) == last

    def send_row(j):
        start, count = batches[j]
        at = pl.ds(start, count)
        state[j]["row"] = remote(
            r.at[at, pl.ds(8 * face, face), :], r.at[at, pl.ds(0, face), :],
            rfs.at[0, j], rfs.at[1, j], elem=right,
        )
        state[j]["row"].start()

    def over(j, body):
        start, count = batches[j]

        def step(p, carry):
            body(p)
            return carry

        lax.fori_loop(start, start + count, step, 0)

    def early_row(j):
        def body(p):
            line = joined([jnp.where(lately, 0.0, t[p, row(8, b), :]) for b in range(NPT)])
            for b in range(NPT):
                r[p, row(8, b), :] = r[p, row(8, b), :] + line[b]

        over(j, body)
        send_row(j)

    def add_pieces(j):
        start, count = batches[j]
        for copy in pieces[j]:
            copy.wait()
        if start == 0:
            push_copy.wait()
        for p in range(start, start + count):
            for g in range(groups):
                e = g * chunks + last
                if j < final:
                    t[p, pl.ds(face + e, rows1, stride=elems), :] = ret1[g, p, :, :]
                else:
                    t[p, pl.ds(e, N2, stride=elems), :] = retw[g, p - wide, :, :]
        if j == final:
            state[j]["row"].wait()

        def body(p):
            for a in range(1 if j < final else 0, NPT):
                line = [t[p, row(a, b), :] for b in range(NPT)]
                if j == final and a in (0, 8):
                    line = [jnp.where(lately, x, 0.0) for x in line]
                if start == 0:
                    push = pjout[...] if a < 8 else pjout[...] + pjin[...]
                    push = push * tk_ref[slot, pl.ds(p, 1), :]
                    line = [line[b] + push * (w[a] * w[b]) for b in range(NPT)]
                line = joined(line)
                for b in range(NPT):
                    r[p, row(a, b), :] = r[p, row(a, b), :] + line[b]

        over(j, body)
        if j < final:
            send_row(j)

    def all_dots(n, i):
        return [
            remote(
                dots.at[n, i], gathered.at[n, i, k - 1], ds.at[n, i, k - 1], dr.at[n, i, k - 1],
                elem=lax.rem(me + k, peers),
            )
            for k in range(1, peers)
        ]

    def total_dots(n, i):
        total = dots[n, i]
        for k in range(peers - 1):
            total = total + gathered[n, i, k]
        return total

    def apply_first(i):
        start, count = batches[i]
        if i < final:
            state[i]["row"].wait()
        dots[0, i] = jnp.ones((4, modes), f32)

        def body(p):
            mf, rx, ry = mf_ref[...], rx_ref[...], ry_ref[...]
            for b in range(NPT):
                v = [r[p, row(a, b), :] for a in range(NPT)]
                kx = line_product(v, even, odd)
                rxb = rx * w[b]
                mfb = mf * w[b]
                for a in range(NPT):
                    qb[p, row(a, b), :] = (mfb * w[a]) * v[a] + rxb * kx[a]
            rr = jnp.zeros((elems, modes), f32)
            pq = jnp.zeros((elems, modes), f32)
            for a in range(NPT):
                v = [r[p, row(a, b), :] for b in range(NPT)]
                ky = line_product(v, even, odd)
                rya = ry * w[a]
                line = [qb[p, row(a, b), :] + rya * ky[b] for b in range(NPT)]
                for b in range(NPT):
                    rr = rr + (mult[a] * mult[b]) * (v[b] * v[b])
                    pq = pq + v[b] * line[b]
                line = joined(line)
                for b in range(NPT):
                    qb[p, row(a, b), :] = line[b]
            dots[0, i, pl.ds(p - start, 1), :] = squash(rr)
            dots[0, i, pl.ds(2 + p - start, 1), :] = squash(pq)

        over(i, body)
        at = pl.ds(start, count)
        faces = [
            remote(
                qb.at[at, pl.ds(8 * face, face), :], from_left.at[at], qfs.at[0, i], qfr.at[0, i],
                elem=right,
            ),
            remote(
                qb.at[at, pl.ds(0, face), :], from_right.at[at], qfs.at[1, i], qfr.at[1, i],
                elem=left,
            ),
        ]
        sums = all_dots(0, i)
        for copy in faces + sums:
            copy.start()
        state[i]["faces"] = faces
        state[i]["sums"] = sums

    def apply_second(i):
        start, count = batches[i]
        for copy in state[i]["sums"] + state[i]["faces"]:
            copy.wait()
        total = total_dots(0, i)
        norm = total[0:2]
        alpha = norm / total[2:4]
        state[i]["norm"], state[i]["alpha"] = norm, alpha
        coef[i, 0:2, :] = alpha
        dots[1, i] = jnp.ones((4, modes), f32)
        here = pl.ds(start, count)
        for at, extra in ((0, from_left), (8 * face, from_right)):
            qb[here, pl.ds(at, face), :] = qb[here, pl.ds(at, face), :] + extra[here]

        def body(p):
            mf, rx, ry = mf_ref[...], rx_ref[...], ry_ref[...]
            al = coef[i, pl.ds(p - start, 1), :]
            rz = jnp.zeros((elems, modes), f32)
            rr = jnp.zeros((elems, modes), f32)
            for b in range(NPT):
                v = [r[p, row(a, b), :] - al * qb[p, row(a, b), :] for a in range(NPT)]
                kx = line_product(v, even, odd)
                one = jnp.zeros((elems, modes), f32)
                two = jnp.zeros((elems, modes), f32)
                for a in range(NPT):
                    qb[p, row(a, b), :] = v[a]
                    square = v[a] * v[a]
                    one = one + v[a] * kx[a]
                    two = two + w[a] * square
                    rr = rr + (mult[a] * mult[b]) * square
                rz = rz + w[b] * (rx * one + mf * two)
            for a in range(NPT):
                v = [qb[p, row(a, b), :] for b in range(NPT)]
                ky = line_product(v, even, odd)
                one = jnp.zeros((elems, modes), f32)
                for b in range(NPT):
                    one = one + v[b] * ky[b]
                rz = rz + (w[a] * ry) * one
            dots[1, i, pl.ds(p - start, 1), :] = squash(rr)
            dots[1, i, pl.ds(2 + p - start, 1), :] = squash(rz)

        over(i, body)
        sums = all_dots(1, i)
        for copy in sums:
            copy.start()
        state[i]["later"] = sums

    def finish(i):
        for copy in state[i]["later"]:
            copy.wait()
        later = total_dots(1, i)
        norm, alpha = state[i]["norm"], state[i]["alpha"]
        following = later[0:2]
        beta = following / norm
        second = following / (later[2:4] - beta * following / alpha)
        first = alpha + second * beta
        start, count = batches[i]
        for p in range(start, start + count):
            n = p - start
            one, two = first[n : n + 1], second[n : n + 1]
            for e in range(elems):
                at = pl.ds(e, N2, stride=elems)
                outv[p // 2, pl.ds(2 * N2 * e + p % 2, N2, stride=2), :] = (
                    one * r[p, at, :] + two * qb[p, at, :]
                )
            ready.append(p)
            if p ^ 1 in ready:
                copy = pltpu.make_async_copy(outv.at[p // 2], out_hbm.at[p // 2], os.at[p // 2])
                copy.start()
                outgoing.append(copy)

    ready, outgoing = [], []
    state = [{} for _ in batches]
    early_row(final)
    stages = {"A": add_pieces, "B": apply_first, "C": apply_second, "D": finish}
    for name, j in zip(order[::2], order[1::2]):
        stages[name](int(j))
    for copy in outgoing:
        copy.wait()


def deliver(source, target, sem):
    copy = pltpu.make_async_copy(source, target, sem)
    copy.start()
    copy.wait()


def window(vel, scalars, tables, groups):
    _, nodes, _, modes = vel.shape
    elems = nodes // N2
    chunks = elems // groups
    count = groups * modes
    half = 3 * count // 2
    tile = tables[1].shape[1]
    peers = lax.axis_size("elem")
    body = lambda *refs: window_kernel(chunks, groups, elems, modes, peers, tile, *refs)
    anywhere = pl.BlockSpec(memory_space=pl.ANY)
    dma = pltpu.SemaphoreType.DMA
    face = NPT * elems
    field = pltpu.VMEM((6, N2 * elems, modes), f32)
    table = pltpu.VMEM((half // tile, count, tile), bf16)
    small = pltpu.VMEM((elems, modes), f32)
    wide = pltpu.VMEM((6 * PAD, count), bf16)
    rows0, rows1 = 8 * (NPT - 1), NPT * (NPT - 1)
    parts = len(batches)
    wide_count = batches[-1][1]
    early = max(chunks - 1, 1)
    prow = -(-chunks // 8) * 8
    result = pl.pallas_call(
        body,
        out_shape=jax.ShapeDtypeStruct((3, 2 * nodes, modes), f32),
        in_specs=[pl.BlockSpec(memory_space=pltpu.HBM)] * (len(tables) + 4),
        out_specs=anywhere,
        scratch_shapes=[pltpu.SMEM(x.shape, x.dtype) for x in scalars]
        + [pltpu.VMEM((3, nodes, 2, modes), f32)]
        + [pltpu.VMEM(x.shape, x.dtype) for x in tables]
        + [
            dma((len(tables) + 4 + chunks,)),
            pltpu.VMEM((chunks, groups, 3, N2, 2, modes), f32),
            dma((chunks, groups - 1)),
            dma((chunks, groups - 1)),
            pltpu.VMEM((chunks, 2, 3 * PAD, count), f32),
            pltpu.VMEM((chunks, 6 * NPT, count), f32),
            pltpu.VMEM((chunks, 6 * NPT, count), f32),
            dma((chunks,)),
            dma((chunks,)),
            pltpu.VMEM((early, groups, 6, rows0, modes), f32),
            pltpu.VMEM((early, groups, 6, rows0, modes), f32),
            pltpu.VMEM((groups, 6 - wide_count, rows1, modes), f32),
            pltpu.VMEM((groups, 6 - wide_count, rows1, modes), f32),
            pltpu.VMEM((groups, wide_count, N2, modes), f32),
            pltpu.VMEM((groups, wide_count, N2, modes), f32),
            dma((early, groups - 1)),
            dma((early, groups - 1)),
            dma((parts, groups - 1)),
            dma((parts, groups - 1)),
            pltpu.VMEM((wide_count * NPT, count), f32),
            pltpu.VMEM((wide_count * NPT, count), f32),
            dma((2,)),
            pltpu.VMEM((prow, modes), f32),
            pltpu.VMEM((groups, prow, modes), f32),
            dma((groups - 1,)),
            dma((groups - 1,)),
            small,
            small,
            dma((2,)),
            field,
            field,
            field,
            pltpu.VMEM((6, face, modes), f32),
            pltpu.VMEM((6, face, modes), f32),
            dma((2,)),
            dma((2, parts)),
            pltpu.VMEM((6, face, modes), f32),
            pltpu.VMEM((6, face, modes), f32),
            dma((2, parts)),
            dma((2, parts)),
            pltpu.VMEM((2, parts, 4, modes), f32),
            pltpu.VMEM((2, parts, peers - 1, 4, modes), f32),
            dma((2, parts, peers - 1)),
            dma((2, parts, peers - 1)),
            pltpu.VMEM((parts, 2, modes), f32),
            pltpu.VMEM((3, 2 * nodes, modes), f32),
            dma((3,)),
            table,
            table,
            table,
            table,
        ]
        + [small] * 6
        + [
            pltpu.VMEM((6 * PAD, count), f32),
            pltpu.VMEM((6 * PAD, count), f32),
            wide,
            wide,
            wide,
            wide,
            pltpu.VMEM((6 * PAD, 128), f32),
            pltpu.VMEM((PAD, tile), f32),
        ],
        compiler_params=pltpu.CompilerParams(
            collective_id=0, has_side_effects=True, vmem_limit_bytes=40 << 20
        ),
    )(scalars[0], *[pltpu.with_memory_space_constraint(x, pltpu.HBM) for x in (*scalars[1:], vel, *tables)])
    return pl.pallas_call(
        deliver,
        out_shape=jax.ShapeDtypeStruct((3, 2 * nodes, modes), f32),
        in_specs=[anywhere],
        out_specs=pl.BlockSpec(memory_space=pltpu.HBM),
        scratch_shapes=[dma],
        compiler_params=pltpu.CompilerParams(vmem_limit_bytes=1 << 20),
    )(result)


def on_device(velocity, column_width, row_height, disc_mask):
    groups = lax.axis_size("mode")
    _, nodes, _, modes = velocity.shape
    count = groups * modes
    planes = 3 * count
    half = planes // 2
    derivative = derivative_matrix()
    stacked = np.zeros((2 * PAD, PAD))
    stacked[:N2, :N2] = np.kron(derivative, np.eye(9))
    stacked[PAD : PAD + N2, :N2] = np.kron(np.eye(9), derivative)
    grads = split_host(stacked)
    host_k = np.arange(count)
    weight = np.where(host_k == 0, 1.0, 2.0) / math.sqrt(count)
    wk = np.zeros((8, count), np.float32)
    wk[0] = weight
    wk[1] = weight * (8.0 / count) * host_k
    wk[2] = 1.0 - 2.0 * (host_k % 2)
    wk = jnp.asarray(wk)
    w = np.array(gll_weights)
    tile = 256 if half % 256 == 0 else half
    w2 = np.zeros((PAD, 1), np.float32)
    w2[:N2, 0] = (w[:, None] * w[None, :]).reshape(-1)
    w2 = jnp.asarray(w2)

    turn = 2.0 * np.pi / planes
    base = turn * (host_k[:, None] * np.arange(tile)[None, :] % planes)
    steps = turn * (host_k[:, None] * tile * np.arange(half // tile)[None, :] % planes)
    rotation = np.stack([np.cos(steps), np.sin(steps)], axis=2).reshape(count, -1)
    tables = tuple(jnp.asarray(t.astype(np.float32)) for t in (np.cos(base), np.sin(base), rotation))
    tables = tables + grads + (wk, w2)
    in_planes = np.arange(3 * planes // 8, 5 * planes // 8)
    arg = 2.0 * np.pi * ((host_k[:, None] * in_planes[None, :]) % planes) / planes
    profile = math.sqrt(count) / planes * np.stack([np.cos(arg).sum(1), -np.sin(arg).sum(1)])
    profile = np.concatenate([profile, np.zeros((6, count))])
    profile = profile.astype(np.float32).reshape(8, groups, modes).transpose(1, 0, 2)
    tables = (jnp.asarray(profile),) + tables
    result = window(velocity, (column_width, row_height, disc_mask), tables, groups)
    return result.reshape(3, nodes, 2, modes)


def solution(mesh):
    return jax.shard_map(
        on_device,
        mesh=mesh,
        in_specs=(P(None, "elem", None, "mode"), P("elem"), P(), P("elem")),
        out_specs=P(None, "elem", None, "mode"),
        check_vma=False,
    )
```

```python
import math

import jax
import jax.numpy as jnp
import numpy as np
from jax import lax
from jax.experimental import pallas as pl
from jax.experimental.pallas import tpu as pltpu
from jax.sharding import PartitionSpec as P

ORDER = 8
NPT = 9
N2 = 81
PAD = 88

gll_points = [
    -1.0,
    -0.8997579954114602,
    -0.6771862795107377,
    -0.3631174638261782,
    0.0,
    0.3631174638261782,
    0.6771862795107377,
    0.8997579954114602,
    1.0,
]
gll_weights = [
    0.0277777777777778,
    0.1654953615608055,
    0.2745387125001617,
    0.3464285109730463,
    0.3715192743764172,
    0.3464285109730463,
    0.2745387125001617,
    0.1654953615608055,
    0.0277777777777778,
]
viscosity = 0.5
time_step = 0.02
thrust_coef = 4.0 / 3.0
f32 = jnp.float32
bf16 = jnp.bfloat16


def derivative_matrix():
    points = np.array(gll_points)
    identity = np.eye(9)
    differences = points[:, None] - points[None, :] + identity
    barycentric = 1.0 / np.prod(differences, axis=1)
    off_diagonal = barycentric[None, :] / barycentric[:, None] / differences * (1.0 - identity)
    return off_diagonal - identity * off_diagonal.sum(axis=1)[:, None]


def split_host(table):
    import ml_dtypes

    high = table.astype(np.float32).astype(ml_dtypes.bfloat16)
    low = (table - high.astype(np.float64)).astype(np.float32).astype(ml_dtypes.bfloat16)
    return jnp.asarray(high), jnp.asarray(low)


def split(x):
    high = x.astype(bf16)
    return high, (x - high.astype(f32)).astype(bf16)


def dot(a, b):
    return jnp.dot(a, b, preferred_element_type=f32)


def dot_nt(a, b):
    return lax.dot_general(a, b, (((1,), (1,)), ((), ())), preferred_element_type=f32)


def dot3(a, b, d=dot):
    return d(a[0], b[0]) + d(a[0], b[1]) + d(a[1], b[0])


def advect_chunk(groups, modes, tile, planes, scales, x, acc_re, acc_im, small, tabs, scratch):
    ghi, glo, wk, w2 = small
    ch, cl, sh, sl = tabs
    xr, xi, rh, rl, ih, il, col0, press = scratch
    half = planes // 2
    for g in range(groups):
        lanes = slice(g * modes, (g + 1) * modes)
        cw = wk[0:1, lanes]
        ck = wk[1:2, lanes]
        for i in range(3):
            start = (3 * g + i) * 2 * N2
            re = x[pl.ds(start, N2, stride=2), :]
            im = x[pl.ds(start + 1, N2, stride=2), :]
            at = slice(PAD * i, PAD * i + N2)
            zt = slice(3 * PAD + PAD * i, 3 * PAD + PAD * i + N2)
            xr[at, lanes] = cw * re
            xi[at, lanes] = cw * im
            xr[zt, lanes] = -ck * im
            xi[zt, lanes] = ck * re
    full = xr[...]
    rh[...], rl[...] = split(full)
    ih[...], il[...] = split(xi[...])
    col0[...] = jnp.broadcast_to(jnp.sum(full * wk[2:3, :], axis=1, keepdims=True), col0.shape)
    acc_re[...] = jnp.zeros(acc_re.shape, f32)
    acc_im[...] = jnp.zeros(acc_im.shape, f32)
    press[...] = jnp.zeros_like(press)

    def step(q, carry):
        ctab = (ch[q], cl[q])
        stab = (sh[q], sl[q])
        cpart = dot3((rh[...], rl[...]), ctab)
        spart = dot3((ih[...], il[...]), stab)
        lane = lax.broadcasted_iota(jnp.int32, (1, tile), 1) + q * tile
        first = lane == 0
        side_a = cpart - spart
        side_b = jnp.where(first, col0[:, 0:1], cpart + spart)
        plane_b = jnp.where(first, half, planes - lane)
        grad = (ghi[...], glo[...])
        tend = []
        total = jnp.zeros((PAD, tile), f32)
        for side, plane in ((side_a, lane), (side_b, plane_b)):
            inside = ((plane >= 3 * planes // 8) & (plane < 5 * planes // 8)).astype(f32)
            u = [side[PAD * i : PAD * i + PAD] for i in range(3)]
            z = [side[3 * PAD + PAD * i : 4 * PAD + PAD * i] for i in range(3)]
            ux = u[0] * scales[0]
            uy = u[1] * scales[1]
            total = total + u[0] * u[0] * inside
            parts = []
            for i in range(3):
                g = dot3(grad, split(u[i]))
                parts.append(-(ux * g[:PAD] + uy * g[PAD:] + u[2] * z[i]))
            tend.append(jnp.concatenate(parts, axis=0))
        press[...] += total * w2[...]
        plus = split(tend[0] + tend[1])
        minus = split(tend[0] - tend[1])
        acc_re[...] += dot3(plus, ctab, dot_nt)
        acc_im[...] -= dot3(minus, stab, dot_nt)

        @pl.when(q == 0)
        def _():
            acc_re[...] += tend[1][:, 0:1] * (wk[2:3, :] - 1.0)

        return carry

    lax.fori_loop(0, half // tile, step, 0)
    return jnp.sum(jnp.sum(press[...], axis=1, keepdims=True), axis=0, keepdims=True)


def partners(me, groups):
    if groups == 4:
        swap = me + 1 - 2 * lax.rem(me, 2)
        return [3 - me, swap, lax.rem(me + 2, 4)]
    return [lax.rem(me + k, groups) for k in range(1, groups)]


def stiffness_line():
    d = derivative_matrix()
    w = np.array(gll_weights)
    k = d.T @ (w[:, None] * d)
    even = np.zeros((5, 5))
    odd = np.zeros((4, 4))
    for i in range(5):
        for j in range(5):
            even[i, j] = k[i, j] if j == 4 else 0.5 * (k[i, j] + k[i, 8 - j])
    for i in range(4):
        for j in range(4):
            odd[i, j] = 0.5 * (k[i, j] - k[i, 8 - j])
    return even, odd


def line_product(v, even, odd):
    s = [v[j] + v[8 - j] for j in range(4)] + [v[4]]
    t = [v[j] - v[8 - j] for j in range(4)]
    ev = [sum(float(even[i, j]) * s[j] for j in range(5)) for i in range(5)]
    od = [sum(float(odd[i, j]) * t[j] for j in range(4)) for i in range(4)]
    return [ev[i] + od[i] for i in range(4)] + [ev[4]] + [ev[i] - od[i] for i in range(3, -1, -1)]


batches = ((0, 2), (2, 2), (4, 2))
order = "A0B0A1C0B1A2B2D0C1C2D1D2"
out_edge, out_inner = "r0s0t0r1s1t1", "r0s0t0r1s1t1"
early_edge, early_inner = "rst", "rst"
late_edge, late_inner = "r0s0t0r1s1t1r2s2t2", "t0s0r0t1s1r1t2s2r2"


def window_kernel(
    chunks, groups, elems, modes, peers, tile,
    hx_hbm, hy_hbm, disc_hbm, vel_hbm, tk_hbm, cb_hbm, sb_hbm, rot_hbm, gh_hbm, gl_hbm, wk_hbm, w2_hbm,
    out_hbm,
    hx_ref, hy_ref, disc_ref, vel, tk_ref, cbase, sbase, rot, ghi, glo, wk, w2, ls,
    recv, rs_out, ss_out, acc, faceout, facein, fxs, fxr,
    spec0, ret0, spec1, ret1, specw, retw, ss0, rs0, ss1, rs1, backout, backin, bks,
    pout, pin, pss, psr, pjout, pjin, pjs,
    r, qb, t, vfout, vfin, vfs, rfs, from_left, from_right, qfs, qfr,
    dots, gathered, ds, dr, coef, partial, outv, os,
    ch, cl, sh, sl, mf_ref, rx_ref, ry_ref, jw_ref, cw_ref, th_ref, *scratch,
):
    me = lax.axis_index("elem")
    slot = lax.axis_index("mode")
    planes = 3 * groups * modes
    face = NPT * elems
    w = gll_weights
    even, odd = stiffness_line()
    mult = [0.5] + [1.0] * 7 + [0.5]
    others = partners(slot, groups)
    right, left = lax.rem(me + 1, peers), lax.rem(me + peers - 1, peers)
    last = chunks - 1
    rows1 = NPT * (NPT - 1)
    mesh_id = pl.DeviceIdType.MESH
    final = len(batches) - 1
    wide = batches[final][0]

    barrier = pltpu.get_barrier_semaphore()
    for other in others:
        pl.semaphore_signal(barrier, inc=1, device_id={"mode": other}, device_id_type=mesh_id)
    for k in range(1, peers):
        pl.semaphore_signal(
            barrier, inc=1, device_id={"elem": lax.rem(me + k, peers)}, device_id_type=mesh_id
        )

    local = [
        pltpu.make_async_copy(source, target, ls.at[n])
        for n, (source, target) in enumerate(
            (
                (cb_hbm, cbase), (sb_hbm, sbase), (rot_hbm, rot), (tk_hbm, tk_ref), (gh_hbm, ghi),
                (gl_hbm, glo), (wk_hbm, wk), (w2_hbm, w2), (vel_hbm, vel),
                (hx_hbm, hx_ref), (hy_hbm, hy_ref), (disc_hbm, disc_ref),
            )
        )
    ]

    def element(owner, c):
        return vel_hbm.at[:, pl.ds((owner * chunks + c) * N2, N2)]

    own = [
        pltpu.make_async_copy(element(slot, c), recv.at[c, slot], ls.at[len(local) + c])
        for c in range(chunks)
    ]
    for copy in local + own:
        copy.start()

    pl.semaphore_wait(barrier, peers - 1 + groups - 1)

    def remote(source, target, send, receive, **where):
        return pltpu.make_async_remote_copy(
            src_ref=source, dst_ref=target, send_sem=send, recv_sem=receive,
            device_id=where, device_id_type=mesh_id,
        )

    outward = [
        [
            remote(element(other, c), recv.at[c, slot], ss_out.at[c, k], rs_out.at[c, k], mode=other)
            for k, other in enumerate(others)
        ]
        for c in range(chunks)
    ]
    edge = (slot == 0) | (slot == groups - 1)

    def launch(copies, edge_order, inner_order):
        if groups != 4 or len(edge_order) != 6 * len(copies):
            for some in copies:
                for copy in some:
                    copy.start()
            return
        for here, text in ((edge, edge_order), (jnp.logical_not(edge), inner_order)):

            @pl.when(here)
            def _():
                for k, j in zip(text[::2], text[1::2]):
                    copies[int(j)]["rst".index(k)].start()

    launch(outward, out_edge, out_inner)

    shape = (elems, modes)
    for copy in local:
        copy.wait()
    for e in range(elems):
        mf_ref[e : e + 1, :] = jnp.full((1, modes), hy_ref[e], f32)
        cw_ref[e : e + 1, :] = jnp.full((1, modes), disc_ref[e], jnp.int32).astype(f32)
    hx, hy, disc = jnp.full(shape, hx_ref[0], f32), mf_ref[...], cw_ref[...]
    index = slot * modes + lax.broadcasted_iota(jnp.int32, shape, 1)
    kz = 8.0 / (groups * modes) * index.astype(f32)
    jacobian = hx * hy / 4.0
    disc_planes = 5 * planes // 8 - 3 * planes // 8
    area = disc_planes * hx * jnp.sum(disc * hy, axis=0, keepdims=True)
    mf_ref[...] = jacobian * (1.0 / time_step + viscosity * kz * kz)
    rx_ref[...] = viscosity * hy / hx
    ry_ref[...] = viscosity * hx / hy
    jw_ref[...] = jacobian / time_step
    cw_ref[...] = disc * jacobian
    th_ref[...] = -(0.5 * thrust_coef * ORDER * time_step) / hx * disc / area

    def row(a, b):
        return pl.ds((a * NPT + b) * elems, elems)

    def joined(line):
        top = line[8] + pltpu.roll(line[0], elems - 1, 0)
        return [pltpu.roll(top, 1, 0)] + line[1:8] + [top]

    xr, xi = scratch[0], scratch[1]
    xr[...] = jnp.zeros_like(xr)
    xi[...] = jnp.zeros_like(xi)
    cos0, sin0 = cbase[...], sbase[...]
    for q in range(planes // 2 // tile):
        cq, sq = rot[:, 2 * q : 2 * q + 1], rot[:, 2 * q + 1 : 2 * q + 2]
        ch[q], cl[q] = split(cos0 * cq - sin0 * sq)
        sh[q], sl[q] = split(sin0 * cq + cos0 * sq)

    mine = vel.reshape(3 * elems * N2 * 2, modes)
    for i in range(3):
        for part in range(2):
            for e in range(elems):
                qb[2 * i + part, pl.ds(e, N2, stride=elems), :] = mine[
                    pl.ds((i * elems + e) * 2 * N2 + part, N2, stride=2), :
                ]

    def masses(p, carry):
        jw = jw_ref[...]
        for a in range(NPT):
            line = joined([qb[p, row(a, b), :] * (jw * (w[a] * w[b])) for b in range(NPT)])
            for b in range(NPT):
                if a == 0:
                    vfout[p, row(0, b), :] = line[b]
                else:
                    r[p, row(a, b), :] = line[b]
                    if b == 8:
                        t[p, row(a, b), :] = jnp.zeros(shape, f32)
        return carry

    lax.fori_loop(0, 6, masses, 0)
    early = remote(vfout, vfin, vfs.at[0], vfs.at[1], elem=left)
    early.start()

    def advance(c):
        for copy in outward[c]:
            copy.wait()
        own[c].wait()
        hy_here = hy_ref[slot * chunks + c]
        scales = (
            2.0 / jnp.full((1, tile), hx_ref[0], f32),
            2.0 / jnp.full((1, tile), hy_here, f32),
        )
        whole = advect_chunk(
            groups, modes, tile, planes, scales, recv.at[c].reshape(groups * 6 * N2, modes),
            acc.at[c, 0], acc.at[c, 1], (ghi, glo, wk, w2), (ch, cl, sh, sl), scratch,
        )
        pout[c : c + 1, :] = jnp.broadcast_to(whole, (1, modes))
        coef_here = math.sqrt(groups * modes) / planes / 4.0
        weight = w2[...] * (coef_here * jnp.full((1, 1), hx_ref[0], f32) * jnp.full((1, 1), hy_here, f32))
        for part in range(2):
            for i in range(3):
                here = slice(PAD * i, PAD * i + PAD)
                acc[c, part, here, :] = acc[c, part, here, :] * weight
                if c > 0:
                    for a in range(NPT):
                        at = PAD * i + NPT * a
                        acc[c, part, at : at + 1, :] += acc[c - 1, part, at + 8 : at + 9, :]
                p = 2 * i + part
                faceout[c, NPT * p : NPT * p + NPT, :] = acc[c, part, PAD * i : PAD * i + NPT, :]
                if c == last and p >= wide:
                    at = slice(NPT * (p - wide), NPT * (p - wide) + NPT)
                    backout[at, :] = acc[c, part, PAD * i + 8 * NPT : PAD * i + N2, :]
        sides = [remote(faceout.at[c], facein.at[c], fxs.at[c], fxr.at[c], elem=left)]
        if c == last:
            sides.append(remote(backout, backin, bks.at[0], bks.at[1], elem=right))
        for side in sides:
            side.start()
        return sides

    def finish_side(c, sides):
        for side in sides:
            side.wait()
        for part in range(2):
            for i in range(3):
                p = 2 * i + part
                count = NPT if c == last else 8
                at = slice(PAD * i + 8 * NPT, PAD * i + 8 * NPT + count)
                acc[c, part, at, :] += facein[c, NPT * p : NPT * p + count, :]
                if c == last and p >= wide:
                    at = slice(PAD * i, PAD * i + NPT)
                    acc[c, part, at, :] += backin[NPT * (p - wide) : NPT * (p - wide) + NPT, :]
                for g in range(groups):
                    lanes = slice(g * modes, (g + 1) * modes)
                    if c < last:
                        for a in range(1, NPT):
                            start = PAD * i + NPT * a
                            spec0[c, g, p, 8 * a - 8 : 8 * a, :] = acc[c, part, start : start + 8, lanes]
                    elif p < wide:
                        spec1[g, p, :, :] = acc[c, part, PAD * i + NPT : PAD * i + N2, lanes]
                    else:
                        specw[g, p - wide, :, :] = acc[c, part, PAD * i : PAD * i + N2, lanes]

    returned = []
    for c in range(chunks):
        side = advance(c)
        if c == 0:
            early.wait()
            add = pl.ds(8 * face, face)
            r[:, add, :] = r[:, add, :] + vfin[...]
        if c == last:
            pcopies = [
                remote(pout, pin.at[slot], pss.at[k], psr.at[k], mode=other)
                for k, other in enumerate(others)
            ]
            for copy in pcopies:
                copy.start()
            pin[slot] = pout[...]
        finish_side(c, side)
        if c < last:
            copies = [
                remote(spec0.at[c, other], ret0.at[c, slot], ss0.at[c, k], rs0.at[c, k], mode=other)
                for k, other in enumerate(others)
            ]
            launch([copies], early_edge[0] + "0" + early_edge[1] + "0" + early_edge[2] + "0",
                   early_inner[0] + "0" + early_inner[1] + "0" + early_inner[2] + "0")
            returned.append(copies)
            ret0[c, slot] = spec0[c, slot]
    pieces = []
    for j, (start, count) in enumerate(batches):
        pieces.append([])
        for k, other in enumerate(others):
            if j < final:
                at = pl.ds(start, count)
                source, target = spec1.at[other, at], ret1.at[slot, at]
            else:
                source, target = specw.at[other], retw.at[slot]
            pieces[j].append(remote(source, target, ss1.at[j, k], rs1.at[j, k], mode=other))
    launch(pieces, late_edge, late_inner)
    ret1[slot] = spec1[slot]
    retw[slot] = specw[slot]

    for c in range(last):
        for copy in returned[c]:
            copy.wait()
        for g in range(groups):
            e = g * chunks + c
            for p in range(6):
                for a in range(1, NPT):
                    t[p, pl.ds(a * face + e, 8, stride=elems), :] = ret0[c, g, p, 8 * a - 8 : 8 * a, :]
    for copy in pcopies:
        copy.wait()
    pressure = jnp.zeros((1, modes), f32)
    for e in range(elems):
        c = e % chunks
        pressure = pressure + cw_ref[e : e + 1, :] * pin[e // chunks, c : c + 1, :]
    push_here = th_ref[...] * pressure * jw_ref[...]
    pjout[...] = push_here
    push_copy = remote(pjout, pjin, pjs.at[0], pjs.at[1], elem=left)
    push_copy.start()

    def squash(x):
        return jnp.sum(x, axis=0, keepdims=True)

    lately = lax.rem(lax.broadcasted_iota(jnp.int32, shape, 0), chunks) == last

    def send_row(j):
        start, count = batches[j]
        at = pl.ds(start, count)
        state[j]["row"] = remote(
            r.at[at, pl.ds(8 * face, face), :], r.at[at, pl.ds(0, face), :],
            rfs.at[0, j], rfs.at[1, j], elem=right,
        )
        state[j]["row"].start()

    def over(j, body):
        start, count = batches[j]

        def step(p, carry):
            body(p)
            return carry

        lax.fori_loop(start, start + count, step, 0)

    def early_row(j):
        def body(p):
            line = joined([jnp.where(lately, 0.0, t[p, row(8, b), :]) for b in range(NPT)])
            for b in range(NPT):
                r[p, row(8, b), :] = r[p, row(8, b), :] + line[b]

        over(j, body)
        send_row(j)

    def add_pieces(j):
        start, count = batches[j]
        for copy in pieces[j]:
            copy.wait()
        if start == 0:
            push_copy.wait()
        for p in range(start, start + count):
            for g in range(groups):
                e = g * chunks + last
                if j < final:
                    t[p, pl.ds(face + e, rows1, stride=elems), :] = ret1[g, p, :, :]
                else:
                    t[p, pl.ds(e, N2, stride=elems), :] = retw[g, p - wide, :, :]
        if j == final:
            state[j]["row"].wait()

        def body(p):
            for a in range(1 if j < final else 0, NPT):
                line = [t[p, row(a, b), :] for b in range(NPT)]
                if j == final and a in (0, 8):
                    line = [jnp.where(lately, x, 0.0) for x in line]
                if start == 0:
                    push = pjout[...] if a < 8 else pjout[...] + pjin[...]
                    push = push * tk_ref[slot, pl.ds(p, 1), :]
                    line = [line[b] + push * (w[a] * w[b]) for b in range(NPT)]
                line = joined(line)
                for b in range(NPT):
                    r[p, row(a, b), :] = r[p, row(a, b), :] + line[b]

        over(j, body)
        if j < final:
            send_row(j)

    def all_dots(n, i):
        return [
            remote(
                dots.at[n, i], gathered.at[n, i, k - 1], ds.at[n, i, k - 1], dr.at[n, i, k - 1],
                elem=lax.rem(me + k, peers),
            )
            for k in range(1, peers)
        ]

    def total_dots(n, i):
        total = dots[n, i]
        for k in range(peers - 1):
            total = total + gathered[n, i, k]
        return total

    def apply_first(i):
        start, count = batches[i]
        if i < final:
            state[i]["row"].wait()
        dots[0, i] = jnp.ones((4, modes), f32)

        def body(p):
            mf, rx = mf_ref[...], rx_ref[...]
            for b in range(NPT):
                v = [r[p, row(a, b), :] for a in range(NPT)]
                kx = line_product(v, even, odd)
                rxb = rx * w[b]
                mfb = mf * w[b]
                for a in range(NPT):
                    qb[p, row(a, b), :] = (mfb * w[a]) * v[a] + rxb * kx[a]
            lines(p, (0, 8), jnp.zeros(shape, f32), jnp.zeros(shape, f32), 0)

        def rest(p):
            lines(p, range(1, 8), partial[p, 0], partial[p, 1], 1)

        def lines(p, columns, rr, pq, done):
            ry = ry_ref[...]
            for a in columns:
                v = [r[p, row(a, b), :] for b in range(NPT)]
                ky = line_product(v, even, odd)
                rya = ry * w[a]
                line = [qb[p, row(a, b), :] + rya * ky[b] for b in range(NPT)]
                for b in range(NPT):
                    rr = rr + (mult[a] * mult[b]) * (v[b] * v[b])
                    pq = pq + v[b] * line[b]
                line = joined(line)
                for b in range(NPT):
                    qb[p, row(a, b), :] = line[b]
            if done:
                dots[0, i, pl.ds(p - start, 1), :] = squash(rr)
                dots[0, i, pl.ds(2 + p - start, 1), :] = squash(pq)
            else:
                partial[p, 0] = rr
                partial[p, 1] = pq

        over(i, body)
        at = pl.ds(start, count)
        faces = [
            remote(
                qb.at[at, pl.ds(8 * face, face), :], from_left.at[at], qfs.at[0, i], qfr.at[0, i],
                elem=right,
            ),
            remote(
                qb.at[at, pl.ds(0, face), :], from_right.at[at], qfs.at[1, i], qfr.at[1, i],
                elem=left,
            ),
        ]
        for copy in faces:
            copy.start()
        over(i, rest)
        sums = all_dots(0, i)
        for copy in sums:
            copy.start()
        state[i]["faces"] = faces
        state[i]["sums"] = sums

    def apply_second(i):
        start, count = batches[i]
        for copy in state[i]["sums"] + state[i]["faces"]:
            copy.wait()
        total = total_dots(0, i)
        norm = total[0:2]
        alpha = norm / total[2:4]
        state[i]["norm"], state[i]["alpha"] = norm, alpha
        coef[i, 0:2, :] = alpha
        dots[1, i] = jnp.ones((4, modes), f32)
        here = pl.ds(start, count)
        for at, extra in ((0, from_left), (8 * face, from_right)):
            qb[here, pl.ds(at, face), :] = qb[here, pl.ds(at, face), :] + extra[here]

        def body(p):
            mf, rx, ry = mf_ref[...], rx_ref[...], ry_ref[...]
            al = coef[i, pl.ds(p - start, 1), :]
            rz = jnp.zeros((elems, modes), f32)
            rr = jnp.zeros((elems, modes), f32)
            for b in range(NPT):
                v = [r[p, row(a, b), :] - al * qb[p, row(a, b), :] for a in range(NPT)]
                kx = line_product(v, even, odd)
                one = jnp.zeros((elems, modes), f32)
                two = jnp.zeros((elems, modes), f32)
                for a in range(NPT):
                    qb[p, row(a, b), :] = v[a]
                    square = v[a] * v[a]
                    one = one + v[a] * kx[a]
                    two = two + w[a] * square
                    rr = rr + (mult[a] * mult[b]) * square
                rz = rz + w[b] * (rx * one + mf * two)
            for a in range(NPT):
                v = [qb[p, row(a, b), :] for b in range(NPT)]
                ky = line_product(v, even, odd)
                one = jnp.zeros((elems, modes), f32)
                for b in range(NPT):
                    one = one + v[b] * ky[b]
                rz = rz + (w[a] * ry) * one
            dots[1, i, pl.ds(p - start, 1), :] = squash(rr)
            dots[1, i, pl.ds(2 + p - start, 1), :] = squash(rz)

        over(i, body)
        sums = all_dots(1, i)
        for copy in sums:
            copy.start()
        state[i]["later"] = sums

    def finish(i):
        for copy in state[i]["later"]:
            copy.wait()
        later = total_dots(1, i)
        norm, alpha = state[i]["norm"], state[i]["alpha"]
        following = later[0:2]
        beta = following / norm
        second = following / (later[2:4] - beta * following / alpha)
        first = alpha + second * beta
        start, count = batches[i]
        for p in range(start, start + count):
            n = p - start
            one, two = first[n : n + 1], second[n : n + 1]
            for e in range(elems):
                at = pl.ds(e, N2, stride=elems)
                outv[p // 2, pl.ds(2 * N2 * e + p % 2, N2, stride=2), :] = (
                    one * r[p, at, :] + two * qb[p, at, :]
                )
            ready.append(p)
            if p ^ 1 in ready:
                copy = pltpu.make_async_copy(outv.at[p // 2], out_hbm.at[p // 2], os.at[p // 2])
                copy.start()
                outgoing.append(copy)

    ready, outgoing = [], []
    state = [{} for _ in batches]
    early_row(final)
    stages = {"A": add_pieces, "B": apply_first, "C": apply_second, "D": finish}
    for name, j in zip(order[::2], order[1::2]):
        stages[name](int(j))
    for copy in outgoing:
        copy.wait()


def deliver(source, target, sem):
    copy = pltpu.make_async_copy(source, target, sem)
    copy.start()
    copy.wait()


def window(vel, scalars, tables, groups):
    _, nodes, _, modes = vel.shape
    elems = nodes // N2
    chunks = elems // groups
    count = groups * modes
    half = 3 * count // 2
    tile = tables[1].shape[1]
    peers = lax.axis_size("elem")
    body = lambda *refs: window_kernel(chunks, groups, elems, modes, peers, tile, *refs)
    anywhere = pl.BlockSpec(memory_space=pl.ANY)
    dma = pltpu.SemaphoreType.DMA
    face = NPT * elems
    field = pltpu.VMEM((6, N2 * elems, modes), f32)
    table = pltpu.VMEM((half // tile, count, tile), bf16)
    small = pltpu.VMEM((elems, modes), f32)
    wide = pltpu.VMEM((6 * PAD, count), bf16)
    rows0, rows1 = 8 * (NPT - 1), NPT * (NPT - 1)
    parts = len(batches)
    wide_count = batches[-1][1]
    early = max(chunks - 1, 1)
    prow = -(-chunks // 8) * 8
    result = pl.pallas_call(
        body,
        out_shape=jax.ShapeDtypeStruct((3, 2 * nodes, modes), f32),
        in_specs=[pl.BlockSpec(memory_space=pltpu.HBM)] * (len(tables) + 4),
        out_specs=anywhere,
        scratch_shapes=[pltpu.SMEM(x.shape, x.dtype) for x in scalars]
        + [pltpu.VMEM((3, nodes, 2, modes), f32)]
        + [pltpu.VMEM(x.shape, x.dtype) for x in tables]
        + [
            dma((len(tables) + 4 + chunks,)),
            pltpu.VMEM((chunks, groups, 3, N2, 2, modes), f32),
            dma((chunks, groups - 1)),
            dma((chunks, groups - 1)),
            pltpu.VMEM((chunks, 2, 3 * PAD, count), f32),
            pltpu.VMEM((chunks, 6 * NPT, count), f32),
            pltpu.VMEM((chunks, 6 * NPT, count), f32),
            dma((chunks,)),
            dma((chunks,)),
            pltpu.VMEM((early, groups, 6, rows0, modes), f32),
            pltpu.VMEM((early, groups, 6, rows0, modes), f32),
            pltpu.VMEM((groups, 6 - wide_count, rows1, modes), f32),
            pltpu.VMEM((groups, 6 - wide_count, rows1, modes), f32),
            pltpu.VMEM((groups, wide_count, N2, modes), f32),
            pltpu.VMEM((groups, wide_count, N2, modes), f32),
            dma((early, groups - 1)),
            dma((early, groups - 1)),
            dma((parts, groups - 1)),
            dma((parts, groups - 1)),
            pltpu.VMEM((wide_count * NPT, count), f32),
            pltpu.VMEM((wide_count * NPT, count), f32),
            dma((2,)),
            pltpu.VMEM((prow, modes), f32),
            pltpu.VMEM((groups, prow, modes), f32),
            dma((groups - 1,)),
            dma((groups - 1,)),
            small,
            small,
            dma((2,)),
            field,
            field,
            field,
            pltpu.VMEM((6, face, modes), f32),
            pltpu.VMEM((6, face, modes), f32),
            dma((2,)),
            dma((2, parts)),
            pltpu.VMEM((6, face, modes), f32),
            pltpu.VMEM((6, face, modes), f32),
            dma((2, parts)),
            dma((2, parts)),
            pltpu.VMEM((2, parts, 4, modes), f32),
            pltpu.VMEM((2, parts, peers - 1, 4, modes), f32),
            dma((2, parts, peers - 1)),
            dma((2, parts, peers - 1)),
            pltpu.VMEM((parts, 2, modes), f32),
            pltpu.VMEM((6, 2, elems, modes), f32),
            pltpu.VMEM((3, 2 * nodes, modes), f32),
            dma((3,)),
            table,
            table,
            table,
            table,
        ]
        + [small] * 6
        + [
            pltpu.VMEM((6 * PAD, count), f32),
            pltpu.VMEM((6 * PAD, count), f32),
            wide,
            wide,
            wide,
            wide,
            pltpu.VMEM((6 * PAD, 128), f32),
            pltpu.VMEM((PAD, tile), f32),
        ],
        compiler_params=pltpu.CompilerParams(
            collective_id=0, has_side_effects=True, vmem_limit_bytes=40 << 20
        ),
    )(scalars[0], *[pltpu.with_memory_space_constraint(x, pltpu.HBM) for x in (*scalars[1:], vel, *tables)])
    return pl.pallas_call(
        deliver,
        out_shape=jax.ShapeDtypeStruct((3, 2 * nodes, modes), f32),
        in_specs=[anywhere],
        out_specs=pl.BlockSpec(memory_space=pltpu.HBM),
        scratch_shapes=[dma],
        compiler_params=pltpu.CompilerParams(vmem_limit_bytes=1 << 20),
    )(result)


def on_device(velocity, column_width, row_height, disc_mask):
    groups = lax.axis_size("mode")
    _, nodes, _, modes = velocity.shape
    count = groups * modes
    planes = 3 * count
    half = planes // 2
    derivative = derivative_matrix()
    stacked = np.zeros((2 * PAD, PAD))
    stacked[:N2, :N2] = np.kron(derivative, np.eye(9))
    stacked[PAD : PAD + N2, :N2] = np.kron(np.eye(9), derivative)
    grads = split_host(stacked)
    host_k = np.arange(count)
    weight = np.where(host_k == 0, 1.0, 2.0) / math.sqrt(count)
    wk = np.zeros((8, count), np.float32)
    wk[0] = weight
    wk[1] = weight * (8.0 / count) * host_k
    wk[2] = 1.0 - 2.0 * (host_k % 2)
    wk = jnp.asarray(wk)
    w = np.array(gll_weights)
    tile = 256 if half % 256 == 0 else half
    w2 = np.zeros((PAD, 1), np.float32)
    w2[:N2, 0] = (w[:, None] * w[None, :]).reshape(-1)
    w2 = jnp.asarray(w2)

    turn = 2.0 * np.pi / planes
    base = turn * (host_k[:, None] * np.arange(tile)[None, :] % planes)
    steps = turn * (host_k[:, None] * tile * np.arange(half // tile)[None, :] % planes)
    rotation = np.stack([np.cos(steps), np.sin(steps)], axis=2).reshape(count, -1)
    tables = tuple(jnp.asarray(t.astype(np.float32)) for t in (np.cos(base), np.sin(base), rotation))
    tables = tables + grads + (wk, w2)
    in_planes = np.arange(3 * planes // 8, 5 * planes // 8)
    arg = 2.0 * np.pi * ((host_k[:, None] * in_planes[None, :]) % planes) / planes
    profile = math.sqrt(count) / planes * np.stack([np.cos(arg).sum(1), -np.sin(arg).sum(1)])
    profile = np.concatenate([profile, np.zeros((6, count))])
    profile = profile.astype(np.float32).reshape(8, groups, modes).transpose(1, 0, 2)
    tables = (jnp.asarray(profile),) + tables
    result = window(velocity, (column_width, row_height, disc_mask), tables, groups)
    return result.reshape(3, nodes, 2, modes)


def solution(mesh):
    return jax.shard_map(
        on_device,
        mesh=mesh,
        in_specs=(P(None, "elem", None, "mode"), P("elem"), P(), P("elem")),
        out_specs=P(None, "elem", None, "mode"),
        check_vma=False,
    )
```

```python
import math

import jax
import jax.numpy as jnp
import numpy as np
from jax import lax
from jax.experimental import pallas as pl
from jax.experimental.pallas import tpu as pltpu
from jax.sharding import PartitionSpec as P

ORDER = 8
NPT = 9
N2 = 81
PAD = 88

gll_points = [
    -1.0,
    -0.8997579954114602,
    -0.6771862795107377,
    -0.3631174638261782,
    0.0,
    0.3631174638261782,
    0.6771862795107377,
    0.8997579954114602,
    1.0,
]
gll_weights = [
    0.0277777777777778,
    0.1654953615608055,
    0.2745387125001617,
    0.3464285109730463,
    0.3715192743764172,
    0.3464285109730463,
    0.2745387125001617,
    0.1654953615608055,
    0.0277777777777778,
]
viscosity = 0.5
time_step = 0.02
thrust_coef = 4.0 / 3.0
f32 = jnp.float32
bf16 = jnp.bfloat16


def derivative_matrix():
    points = np.array(gll_points)
    identity = np.eye(9)
    differences = points[:, None] - points[None, :] + identity
    barycentric = 1.0 / np.prod(differences, axis=1)
    off_diagonal = barycentric[None, :] / barycentric[:, None] / differences * (1.0 - identity)
    return off_diagonal - identity * off_diagonal.sum(axis=1)[:, None]


def split_host(table):
    import ml_dtypes

    high = table.astype(np.float32).astype(ml_dtypes.bfloat16)
    low = (table - high.astype(np.float64)).astype(np.float32).astype(ml_dtypes.bfloat16)
    return jnp.asarray(high), jnp.asarray(low)


def split(x):
    high = x.astype(bf16)
    return high, (x - high.astype(f32)).astype(bf16)


def dot(a, b):
    return jnp.dot(a, b, preferred_element_type=f32)


def dot_nt(a, b):
    return lax.dot_general(a, b, (((1,), (1,)), ((), ())), preferred_element_type=f32)


def dot3(a, b, d=dot):
    return d(a[0], b[0]) + d(a[0], b[1]) + d(a[1], b[0])


def advect_chunk(groups, modes, tile, planes, scales, x, acc_re, acc_im, small, tabs, scratch):
    ghi, glo, wk, w2 = small
    ch, cl, sh, sl = tabs
    xr, xi, rh, rl, ih, il, col0, press = scratch
    half = planes // 2
    for g in range(groups):
        lanes = slice(g * modes, (g + 1) * modes)
        cw = wk[0:1, lanes]
        ck = wk[1:2, lanes]
        for i in range(3):
            start = (3 * g + i) * 2 * N2
            re = x[pl.ds(start, N2, stride=2), :]
            im = x[pl.ds(start + 1, N2, stride=2), :]
            at = slice(PAD * i, PAD * i + N2)
            zt = slice(3 * PAD + PAD * i, 3 * PAD + PAD * i + N2)
            xr[at, lanes] = cw * re
            xi[at, lanes] = cw * im
            xr[zt, lanes] = -ck * im
            xi[zt, lanes] = ck * re
    full = xr[...]
    rh[...], rl[...] = split(full)
    ih[...], il[...] = split(xi[...])
    col0[...] = jnp.broadcast_to(jnp.sum(full * wk[2:3, :], axis=1, keepdims=True), col0.shape)
    acc_re[...] = jnp.zeros(acc_re.shape, f32)
    acc_im[...] = jnp.zeros(acc_im.shape, f32)
    press[...] = jnp.zeros_like(press)

    def step(q, carry):
        ctab = (ch[q], cl[q])
        stab = (sh[q], sl[q])
        cpart = dot3((rh[...], rl[...]), ctab)
        spart = dot3((ih[...], il[...]), stab)
        lane = lax.broadcasted_iota(jnp.int32, (1, tile), 1) + q * tile
        first = lane == 0
        side_a = cpart - spart
        side_b = jnp.where(first, col0[:, 0:1], cpart + spart)
        plane_b = jnp.where(first, half, planes - lane)
        grad = (ghi[...], glo[...])
        tend = []
        total = jnp.zeros((PAD, tile), f32)
        for side, plane in ((side_a, lane), (side_b, plane_b)):
            inside = ((plane >= 3 * planes // 8) & (plane < 5 * planes // 8)).astype(f32)
            u = [side[PAD * i : PAD * i + PAD] for i in range(3)]
            z = [side[3 * PAD + PAD * i : 4 * PAD + PAD * i] for i in range(3)]
            ux = u[0] * scales[0]
            uy = u[1] * scales[1]
            total = total + u[0] * u[0] * inside
            parts = []
            for i in range(3):
                g = dot3(grad, split(u[i]))
                parts.append(-(ux * g[:PAD] + uy * g[PAD:] + u[2] * z[i]))
            tend.append(jnp.concatenate(parts, axis=0))
        press[...] += total * w2[...]
        plus = split(tend[0] + tend[1])
        minus = split(tend[0] - tend[1])
        acc_re[...] += dot3(plus, ctab, dot_nt)
        acc_im[...] -= dot3(minus, stab, dot_nt)

        @pl.when(q == 0)
        def _():
            acc_re[...] += tend[1][:, 0:1] * (wk[2:3, :] - 1.0)

        return carry

    lax.fori_loop(0, half // tile, step, 0)
    return jnp.sum(jnp.sum(press[...], axis=1, keepdims=True), axis=0, keepdims=True)


def partners(me, groups):
    if groups == 4:
        swap = me + 1 - 2 * lax.rem(me, 2)
        return [3 - me, swap, lax.rem(me + 2, 4)]
    return [lax.rem(me + k, groups) for k in range(1, groups)]


def stiffness_line():
    d = derivative_matrix()
    w = np.array(gll_weights)
    k = d.T @ (w[:, None] * d)
    even = np.zeros((5, 5))
    odd = np.zeros((4, 4))
    for i in range(5):
        for j in range(5):
            even[i, j] = k[i, j] if j == 4 else 0.5 * (k[i, j] + k[i, 8 - j])
    for i in range(4):
        for j in range(4):
            odd[i, j] = 0.5 * (k[i, j] - k[i, 8 - j])
    return even, odd


def line_product(v, even, odd):
    s = [v[j] + v[8 - j] for j in range(4)] + [v[4]]
    t = [v[j] - v[8 - j] for j in range(4)]
    ev = [sum(float(even[i, j]) * s[j] for j in range(5)) for i in range(5)]
    od = [sum(float(odd[i, j]) * t[j] for j in range(4)) for i in range(4)]
    return [ev[i] + od[i] for i in range(4)] + [ev[4]] + [ev[i] - od[i] for i in range(3, -1, -1)]


batches = ((0, 2), (2, 2), (4, 2))
order = "A0B0A1C0B1A2B2D0C1C2D1D2"
out_edge, out_inner = "r0s0t0r1s1t1", "s0r0t0s1r1t1"
early_edge, early_inner = "rst", "rst"
late_edge, late_inner = "r0s0t0", "t0s0r0"


def window_kernel(
    chunks, groups, elems, modes, peers, tile,
    hx_hbm, hy_hbm, disc_hbm, vel_hbm, tk_hbm, cb_hbm, sb_hbm, rot_hbm, gh_hbm, gl_hbm, wk_hbm, w2_hbm,
    out_hbm,
    hx_ref, hy_ref, disc_ref, vel, tk_ref, cbase, sbase, rot, ghi, glo, wk, w2, ls,
    recv, rs_out, ss_out, acc, faceout, facein, fxs, fxr,
    spec0, ret0, spec1, ret1, specw, retw, ss0, rs0, ss1, rs1, backout, backin, bks,
    pout, pin, pss, psr, pjout, pjin, pjs,
    r, qb, t, vfout, vfin, vfs, rfs, from_left, from_right, qfs, qfr,
    dots, gathered, ds, dr, coef, partial, outv, os,
    ch, cl, sh, sl, mf_ref, rx_ref, ry_ref, jw_ref, cw_ref, th_ref, *scratch,
):
    me = lax.axis_index("elem")
    slot = lax.axis_index("mode")
    planes = 3 * groups * modes
    face = NPT * elems
    w = gll_weights
    even, odd = stiffness_line()
    mult = [0.5] + [1.0] * 7 + [0.5]
    others = partners(slot, groups)
    right, left = lax.rem(me + 1, peers), lax.rem(me + peers - 1, peers)
    last = chunks - 1
    rows1 = NPT * (NPT - 1)
    mesh_id = pl.DeviceIdType.MESH
    final = len(batches) - 1
    wide = batches[final][0]

    barrier = pltpu.get_barrier_semaphore()
    for other in others:
        pl.semaphore_signal(barrier, inc=1, device_id={"mode": other}, device_id_type=mesh_id)
    for k in range(1, peers):
        pl.semaphore_signal(
            barrier, inc=1, device_id={"elem": lax.rem(me + k, peers)}, device_id_type=mesh_id
        )

    local = [
        pltpu.make_async_copy(source, target, ls.at[n])
        for n, (source, target) in enumerate(
            (
                (cb_hbm, cbase), (sb_hbm, sbase), (rot_hbm, rot), (tk_hbm, tk_ref), (gh_hbm, ghi),
                (gl_hbm, glo), (wk_hbm, wk), (w2_hbm, w2), (vel_hbm, vel),
                (hx_hbm, hx_ref), (hy_hbm, hy_ref), (disc_hbm, disc_ref),
            )
        )
    ]

    def element(owner, c):
        return vel_hbm.at[:, pl.ds((owner * chunks + c) * N2, N2)]

    own = [
        pltpu.make_async_copy(element(slot, c), recv.at[c, slot], ls.at[len(local) + c])
        for c in range(chunks)
    ]
    for copy in local + own:
        copy.start()

    pl.semaphore_wait(barrier, peers - 1 + groups - 1)

    def remote(source, target, send, receive, **where):
        return pltpu.make_async_remote_copy(
            src_ref=source, dst_ref=target, send_sem=send, recv_sem=receive,
            device_id=where, device_id_type=mesh_id,
        )

    outward = [
        [
            remote(element(other, c), recv.at[c, slot], ss_out.at[c, k], rs_out.at[c, k], mode=other)
            for k, other in enumerate(others)
        ]
        for c in range(chunks)
    ]
    edge = (slot == 0) | (slot == groups - 1)

    def launch(copies, edge_order, inner_order):
        if groups != 4 or len(edge_order) != 6 * len(copies):
            for some in copies:
                for copy in some:
                    copy.start()
            return
        for here, text in ((edge, edge_order), (jnp.logical_not(edge), inner_order)):

            @pl.when(here)
            def _():
                for k, j in zip(text[::2], text[1::2]):
                    copies[int(j)]["rst".index(k)].start()

    launch(outward, out_edge, out_inner)

    shape = (elems, modes)
    for copy in local:
        copy.wait()
    for e in range(elems):
        mf_ref[e : e + 1, :] = jnp.full((1, modes), hy_ref[e], f32)
        cw_ref[e : e + 1, :] = jnp.full((1, modes), disc_ref[e], jnp.int32).astype(f32)
    hx, hy, disc = jnp.full(shape, hx_ref[0], f32), mf_ref[...], cw_ref[...]
    index = slot * modes + lax.broadcasted_iota(jnp.int32, shape, 1)
    kz = 8.0 / (groups * modes) * index.astype(f32)
    jacobian = hx * hy / 4.0
    disc_planes = 5 * planes // 8 - 3 * planes // 8
    area = disc_planes * hx * jnp.sum(disc * hy, axis=0, keepdims=True)
    mf_ref[...] = jacobian * (1.0 / time_step + viscosity * kz * kz)
    rx_ref[...] = viscosity * hy / hx
    ry_ref[...] = viscosity * hx / hy
    jw_ref[...] = jacobian / time_step
    cw_ref[...] = disc * jacobian
    th_ref[...] = -(0.5 * thrust_coef * ORDER * time_step) / hx * disc / area

    def row(a, b):
        return pl.ds((a * NPT + b) * elems, elems)

    def joined(line):
        top = line[8] + pltpu.roll(line[0], elems - 1, 0)
        return [pltpu.roll(top, 1, 0)] + line[1:8] + [top]

    xr, xi = scratch[0], scratch[1]
    xr[...] = jnp.zeros_like(xr)
    xi[...] = jnp.zeros_like(xi)
    cos0, sin0 = cbase[...], sbase[...]
    for q in range(planes // 2 // tile):
        cq, sq = rot[:, 2 * q : 2 * q + 1], rot[:, 2 * q + 1 : 2 * q + 2]
        ch[q], cl[q] = split(cos0 * cq - sin0 * sq)
        sh[q], sl[q] = split(sin0 * cq + cos0 * sq)

    mine = vel.reshape(3 * elems * N2 * 2, modes)
    for i in range(3):
        for part in range(2):
            for e in range(elems):
                qb[2 * i + part, pl.ds(e, N2, stride=elems), :] = mine[
                    pl.ds((i * elems + e) * 2 * N2 + part, N2, stride=2), :
                ]

    def masses(p, carry):
        jw = jw_ref[...]
        for a in range(NPT):
            line = joined([qb[p, row(a, b), :] * (jw * (w[a] * w[b])) for b in range(NPT)])
            for b in range(NPT):
                if a == 0:
                    vfout[p, row(0, b), :] = line[b]
                else:
                    r[p, row(a, b), :] = line[b]
                    if b == 8:
                        t[p, row(a, b), :] = jnp.zeros(shape, f32)
        return carry

    lax.fori_loop(0, 6, masses, 0)
    early = remote(vfout, vfin, vfs.at[0], vfs.at[1], elem=left)
    early.start()

    def advance(c):
        for copy in outward[c]:
            copy.wait()
        own[c].wait()
        hy_here = hy_ref[slot * chunks + c]
        scales = (
            2.0 / jnp.full((1, tile), hx_ref[0], f32),
            2.0 / jnp.full((1, tile), hy_here, f32),
        )
        whole = advect_chunk(
            groups, modes, tile, planes, scales, recv.at[c].reshape(groups * 6 * N2, modes),
            acc.at[c, 0], acc.at[c, 1], (ghi, glo, wk, w2), (ch, cl, sh, sl), scratch,
        )
        pout[c : c + 1, :] = jnp.broadcast_to(whole, (1, modes))
        coef_here = math.sqrt(groups * modes) / planes / 4.0
        weight = w2[...] * (coef_here * jnp.full((1, 1), hx_ref[0], f32) * jnp.full((1, 1), hy_here, f32))
        for part in range(2):
            for i in range(3):
                here = slice(PAD * i, PAD * i + PAD)
                acc[c, part, here, :] = acc[c, part, here, :] * weight
                if c > 0:
                    for a in range(NPT):
                        at = PAD * i + NPT * a
                        acc[c, part, at : at + 1, :] += acc[c - 1, part, at + 8 : at + 9, :]
                p = 2 * i + part
                faceout[c, NPT * p : NPT * p + NPT, :] = acc[c, part, PAD * i : PAD * i + NPT, :]
                if c == last and p >= wide:
                    at = slice(NPT * (p - wide), NPT * (p - wide) + NPT)
                    backout[at, :] = acc[c, part, PAD * i + 8 * NPT : PAD * i + N2, :]
        sides = [remote(faceout.at[c], facein.at[c], fxs.at[c], fxr.at[c], elem=left)]
        if c == last:
            sides.append(remote(backout, backin, bks.at[0], bks.at[1], elem=right))
        for side in sides:
            side.start()
        return sides

    def finish_side(c, sides):
        for side in sides:
            side.wait()
        for part in range(2):
            for i in range(3):
                p = 2 * i + part
                count = NPT if c == last else 8
                at = slice(PAD * i + 8 * NPT, PAD * i + 8 * NPT + count)
                acc[c, part, at, :] += facein[c, NPT * p : NPT * p + count, :]
                if c == last and p >= wide:
                    at = slice(PAD * i, PAD * i + NPT)
                    acc[c, part, at, :] += backin[NPT * (p - wide) : NPT * (p - wide) + NPT, :]
                for g in range(groups):
                    lanes = slice(g * modes, (g + 1) * modes)
                    if c < last:
                        for a in range(1, NPT):
                            start = PAD * i + NPT * a
                            spec0[c, g, p, 8 * a - 8 : 8 * a, :] = acc[c, part, start : start + 8, lanes]
                    elif p < wide:
                        spec1[g, p, :, :] = acc[c, part, PAD * i + NPT : PAD * i + N2, lanes]
                    else:
                        specw[g, p - wide, :, :] = acc[c, part, PAD * i : PAD * i + N2, lanes]

    returned = []
    for c in range(chunks):
        side = advance(c)
        if c == 0:
            early.wait()
            add = pl.ds(8 * face, face)
            r[:, add, :] = r[:, add, :] + vfin[...]
        if c == last:
            pcopies = [
                remote(pout, pin.at[slot], pss.at[k], psr.at[k], mode=other)
                for k, other in enumerate(others)
            ]
            for copy in pcopies:
                copy.start()
            pin[slot] = pout[...]
        finish_side(c, side)
        if c < last:
            copies = [
                remote(spec0.at[c, other], ret0.at[c, slot], ss0.at[c, k], rs0.at[c, k], mode=other)
                for k, other in enumerate(others)
            ]
            launch([copies], early_edge[0] + "0" + early_edge[1] + "0" + early_edge[2] + "0",
                   early_inner[0] + "0" + early_inner[1] + "0" + early_inner[2] + "0")
            returned.append(copies)
            ret0[c, slot] = spec0[c, slot]
    pieces = []
    for j, (start, count) in enumerate(batches):
        pieces.append([])
        for k, other in enumerate(others):
            if j < final:
                at = pl.ds(start, count)
                source, target = spec1.at[other, at], ret1.at[slot, at]
            else:
                source, target = specw.at[other], retw.at[slot]
            pieces[j].append(remote(source, target, ss1.at[j, k], rs1.at[j, k], mode=other))
    def launch_batch(j):
        launch([pieces[j]], late_edge, late_inner)

    launch_batch(0)
    launch_batch(1)
    ret1[slot] = spec1[slot]
    retw[slot] = specw[slot]

    for c in range(last):
        for copy in returned[c]:
            copy.wait()
    launch_batch(2)
    for c in range(last):
        for g in range(groups):
            e = g * chunks + c
            for p in range(6):
                for a in range(1, NPT):
                    t[p, pl.ds(a * face + e, 8, stride=elems), :] = ret0[c, g, p, 8 * a - 8 : 8 * a, :]
    for copy in pcopies:
        copy.wait()
    pressure = jnp.zeros((1, modes), f32)
    for e in range(elems):
        c = e % chunks
        pressure = pressure + cw_ref[e : e + 1, :] * pin[e // chunks, c : c + 1, :]
    push_here = th_ref[...] * pressure * jw_ref[...]
    pjout[...] = push_here
    push_copy = remote(pjout, pjin, pjs.at[0], pjs.at[1], elem=left)
    push_copy.start()

    def squash(x):
        return jnp.sum(x, axis=0, keepdims=True)

    lately = lax.rem(lax.broadcasted_iota(jnp.int32, shape, 0), chunks) == last

    def send_row(j):
        start, count = batches[j]
        at = pl.ds(start, count)
        state[j]["row"] = remote(
            r.at[at, pl.ds(8 * face, face), :], r.at[at, pl.ds(0, face), :],
            rfs.at[0, j], rfs.at[1, j], elem=right,
        )
        state[j]["row"].start()

    def over(j, body):
        start, count = batches[j]

        def step(p, carry):
            body(p)
            return carry

        lax.fori_loop(start, start + count, step, 0)

    def early_row(j):
        def body(p):
            line = joined([jnp.where(lately, 0.0, t[p, row(8, b), :]) for b in range(NPT)])
            for b in range(NPT):
                r[p, row(8, b), :] = r[p, row(8, b), :] + line[b]

        over(j, body)
        send_row(j)

    def add_pieces(j):
        start, count = batches[j]
        for copy in pieces[j]:
            copy.wait()
        if start == 0:
            push_copy.wait()
        for p in range(start, start + count):
            for g in range(groups):
                e = g * chunks + last
                if j < final:
                    t[p, pl.ds(face + e, rows1, stride=elems), :] = ret1[g, p, :, :]
                else:
                    t[p, pl.ds(e, N2, stride=elems), :] = retw[g, p - wide, :, :]
        if j == final:
            state[j]["row"].wait()

        def body(p):
            for a in range(1 if j < final else 0, NPT):
                line = [t[p, row(a, b), :] for b in range(NPT)]
                if j == final and a in (0, 8):
                    line = [jnp.where(lately, x, 0.0) for x in line]
                if start == 0:
                    push = pjout[...] if a < 8 else pjout[...] + pjin[...]
                    push = push * tk_ref[slot, pl.ds(p, 1), :]
                    line = [line[b] + push * (w[a] * w[b]) for b in range(NPT)]
                line = joined(line)
                for b in range(NPT):
                    r[p, row(a, b), :] = r[p, row(a, b), :] + line[b]

        over(j, body)
        if j < final:
            send_row(j)

    def all_dots(n, i):
        return [
            remote(
                dots.at[n, i], gathered.at[n, i, k - 1], ds.at[n, i, k - 1], dr.at[n, i, k - 1],
                elem=lax.rem(me + k, peers),
            )
            for k in range(1, peers)
        ]

    def total_dots(n, i):
        total = dots[n, i]
        for k in range(peers - 1):
            total = total + gathered[n, i, k]
        return total

    def apply_first(i):
        start, count = batches[i]
        if i < final:
            state[i]["row"].wait()
        dots[0, i] = jnp.ones((4, modes), f32)

        def body(p):
            mf, rx = mf_ref[...], rx_ref[...]
            for b in range(NPT):
                v = [r[p, row(a, b), :] for a in range(NPT)]
                kx = line_product(v, even, odd)
                rxb = rx * w[b]
                mfb = mf * w[b]
                for a in range(NPT):
                    qb[p, row(a, b), :] = (mfb * w[a]) * v[a] + rxb * kx[a]
            lines(p, (0, 8), jnp.zeros(shape, f32), jnp.zeros(shape, f32), 0)

        def rest(p):
            lines(p, range(1, 8), partial[p, 0], partial[p, 1], 1)

        def lines(p, columns, rr, pq, done):
            ry = ry_ref[...]
            for a in columns:
                v = [r[p, row(a, b), :] for b in range(NPT)]
                ky = line_product(v, even, odd)
                rya = ry * w[a]
                line = [qb[p, row(a, b), :] + rya * ky[b] for b in range(NPT)]
                for b in range(NPT):
                    rr = rr + (mult[a] * mult[b]) * (v[b] * v[b])
                    pq = pq + v[b] * line[b]
                line = joined(line)
                for b in range(NPT):
                    qb[p, row(a, b), :] = line[b]
            if done:
                dots[0, i, pl.ds(p - start, 1), :] = squash(rr)
                dots[0, i, pl.ds(2 + p - start, 1), :] = squash(pq)
            else:
                partial[p, 0] = rr
                partial[p, 1] = pq

        over(i, body)
        at = pl.ds(start, count)
        faces = [
            remote(
                qb.at[at, pl.ds(8 * face, face), :], from_left.at[at], qfs.at[0, i], qfr.at[0, i],
                elem=right,
            ),
            remote(
                qb.at[at, pl.ds(0, face), :], from_right.at[at], qfs.at[1, i], qfr.at[1, i],
                elem=left,
            ),
        ]
        for copy in faces:
            copy.start()
        over(i, rest)
        sums = all_dots(0, i)
        for copy in sums:
            copy.start()
        state[i]["faces"] = faces
        state[i]["sums"] = sums

    def apply_second(i):
        start, count = batches[i]
        for copy in state[i]["sums"]:
            copy.wait()
        total = total_dots(0, i)
        norm = total[0:2]
        alpha = norm / total[2:4]
        state[i]["norm"], state[i]["alpha"] = norm, alpha
        coef[i, 0:2, :] = alpha
        dots[1, i] = jnp.ones((4, modes), f32)
        here = pl.ds(start, count)
        for copy in state[i]["faces"]:
            copy.wait()
        for at, extra in ((0, from_left), (8 * face, from_right)):
            qb[here, pl.ds(at, face), :] = qb[here, pl.ds(at, face), :] + extra[here]

        def body(p):
            mf, rx, ry = mf_ref[...], rx_ref[...], ry_ref[...]
            al = coef[i, pl.ds(p - start, 1), :]
            rz = jnp.zeros((elems, modes), f32)
            rr = jnp.zeros((elems, modes), f32)
            for b in range(NPT):
                v = [r[p, row(a, b), :] - al * qb[p, row(a, b), :] for a in range(NPT)]
                kx = line_product(v, even, odd)
                one = jnp.zeros((elems, modes), f32)
                two = jnp.zeros((elems, modes), f32)
                for a in range(NPT):
                    qb[p, row(a, b), :] = v[a]
                    square = v[a] * v[a]
                    one = one + v[a] * kx[a]
                    two = two + w[a] * square
                    rr = rr + (mult[a] * mult[b]) * square
                rz = rz + w[b] * (rx * one + mf * two)
            for a in range(NPT):
                v = [qb[p, row(a, b), :] for b in range(NPT)]
                ky = line_product(v, even, odd)
                one = jnp.zeros((elems, modes), f32)
                for b in range(NPT):
                    one = one + v[b] * ky[b]
                rz = rz + (w[a] * ry) * one
            dots[1, i, pl.ds(p - start, 1), :] = squash(rr)
            dots[1, i, pl.ds(2 + p - start, 1), :] = squash(rz)

        over(i, body)
        sums = all_dots(1, i)
        for copy in sums:
            copy.start()
        state[i]["later"] = sums

    def finish(i):
        for copy in state[i]["later"]:
            copy.wait()
        later = total_dots(1, i)
        norm, alpha = state[i]["norm"], state[i]["alpha"]
        following = later[0:2]
        beta = following / norm
        second = following / (later[2:4] - beta * following / alpha)
        first = alpha + second * beta
        start, count = batches[i]
        for p in range(start, start + count):
            n = p - start
            one, two = first[n : n + 1], second[n : n + 1]
            for e in range(elems):
                at = pl.ds(e, N2, stride=elems)
                outv[p // 2, pl.ds(2 * N2 * e + p % 2, N2, stride=2), :] = (
                    one * r[p, at, :] + two * qb[p, at, :]
                )
            ready.append(p)
            if p ^ 1 in ready:
                copy = pltpu.make_async_copy(outv.at[p // 2], out_hbm.at[p // 2], os.at[p // 2])
                copy.start()
                outgoing.append(copy)

    ready, outgoing = [], []
    state = [{} for _ in batches]
    early_row(final)
    stages = {"A": add_pieces, "B": apply_first, "C": apply_second, "D": finish}
    for name, j in zip(order[::2], order[1::2]):
        stages[name](int(j))
    for copy in outgoing:
        copy.wait()


def deliver(source, target, sem):
    copy = pltpu.make_async_copy(source, target, sem)
    copy.start()
    copy.wait()


def window(vel, scalars, tables, groups):
    _, nodes, _, modes = vel.shape
    elems = nodes // N2
    chunks = elems // groups
    count = groups * modes
    half = 3 * count // 2
    tile = tables[1].shape[1]
    peers = lax.axis_size("elem")
    body = lambda *refs: window_kernel(chunks, groups, elems, modes, peers, tile, *refs)
    anywhere = pl.BlockSpec(memory_space=pl.ANY)
    dma = pltpu.SemaphoreType.DMA
    face = NPT * elems
    field = pltpu.VMEM((6, N2 * elems, modes), f32)
    table = pltpu.VMEM((half // tile, count, tile), bf16)
    small = pltpu.VMEM((elems, modes), f32)
    wide = pltpu.VMEM((6 * PAD, count), bf16)
    rows0, rows1 = 8 * (NPT - 1), NPT * (NPT - 1)
    parts = len(batches)
    wide_count = batches[-1][1]
    early = max(chunks - 1, 1)
    prow = -(-chunks // 8) * 8
    result = pl.pallas_call(
        body,
        out_shape=jax.ShapeDtypeStruct((3, 2 * nodes, modes), f32),
        in_specs=[pl.BlockSpec(memory_space=pltpu.HBM)] * (len(tables) + 4),
        out_specs=anywhere,
        scratch_shapes=[pltpu.SMEM(x.shape, x.dtype) for x in scalars]
        + [pltpu.VMEM((3, nodes, 2, modes), f32)]
        + [pltpu.VMEM(x.shape, x.dtype) for x in tables]
        + [
            dma((len(tables) + 4 + chunks,)),
            pltpu.VMEM((chunks, groups, 3, N2, 2, modes), f32),
            dma((chunks, groups - 1)),
            dma((chunks, groups - 1)),
            pltpu.VMEM((chunks, 2, 3 * PAD, count), f32),
            pltpu.VMEM((chunks, 6 * NPT, count), f32),
            pltpu.VMEM((chunks, 6 * NPT, count), f32),
            dma((chunks,)),
            dma((chunks,)),
            pltpu.VMEM((early, groups, 6, rows0, modes), f32),
            pltpu.VMEM((early, groups, 6, rows0, modes), f32),
            pltpu.VMEM((groups, 6 - wide_count, rows1, modes), f32),
            pltpu.VMEM((groups, 6 - wide_count, rows1, modes), f32),
            pltpu.VMEM((groups, wide_count, N2, modes), f32),
            pltpu.VMEM((groups, wide_count, N2, modes), f32),
            dma((early, groups - 1)),
            dma((early, groups - 1)),
            dma((parts, groups - 1)),
            dma((parts, groups - 1)),
            pltpu.VMEM((wide_count * NPT, count), f32),
            pltpu.VMEM((wide_count * NPT, count), f32),
            dma((2,)),
            pltpu.VMEM((prow, modes), f32),
            pltpu.VMEM((groups, prow, modes), f32),
            dma((groups - 1,)),
            dma((groups - 1,)),
            small,
            small,
            dma((2,)),
            field,
            field,
            field,
            pltpu.VMEM((6, face, modes), f32),
            pltpu.VMEM((6, face, modes), f32),
            dma((2,)),
            dma((2, parts)),
            pltpu.VMEM((6, face, modes), f32),
            pltpu.VMEM((6, face, modes), f32),
            dma((2, parts)),
            dma((2, parts)),
            pltpu.VMEM((2, parts, 4, modes), f32),
            pltpu.VMEM((2, parts, peers - 1, 4, modes), f32),
            dma((2, parts, peers - 1)),
            dma((2, parts, peers - 1)),
            pltpu.VMEM((parts, 2, modes), f32),
            pltpu.VMEM((6, 2, elems, modes), f32),
            pltpu.VMEM((3, 2 * nodes, modes), f32),
            dma((3,)),
            table,
            table,
            table,
            table,
        ]
        + [small] * 6
        + [
            pltpu.VMEM((6 * PAD, count), f32),
            pltpu.VMEM((6 * PAD, count), f32),
            wide,
            wide,
            wide,
            wide,
            pltpu.VMEM((6 * PAD, 128), f32),
            pltpu.VMEM((PAD, tile), f32),
        ],
        compiler_params=pltpu.CompilerParams(
            collective_id=0, has_side_effects=True, vmem_limit_bytes=40 << 20
        ),
    )(scalars[0], *[pltpu.with_memory_space_constraint(x, pltpu.HBM) for x in (*scalars[1:], vel, *tables)])
    return pl.pallas_call(
        deliver,
        out_shape=jax.ShapeDtypeStruct((3, 2 * nodes, modes), f32),
        in_specs=[anywhere],
        out_specs=pl.BlockSpec(memory_space=pltpu.HBM),
        scratch_shapes=[dma],
        compiler_params=pltpu.CompilerParams(vmem_limit_bytes=1 << 20),
    )(result)


def on_device(velocity, column_width, row_height, disc_mask):
    groups = lax.axis_size("mode")
    _, nodes, _, modes = velocity.shape
    count = groups * modes
    planes = 3 * count
    half = planes // 2
    derivative = derivative_matrix()
    stacked = np.zeros((2 * PAD, PAD))
    stacked[:N2, :N2] = np.kron(derivative, np.eye(9))
    stacked[PAD : PAD + N2, :N2] = np.kron(np.eye(9), derivative)
    grads = split_host(stacked)
    host_k = np.arange(count)
    weight = np.where(host_k == 0, 1.0, 2.0) / math.sqrt(count)
    wk = np.zeros((8, count), np.float32)
    wk[0] = weight
    wk[1] = weight * (8.0 / count) * host_k
    wk[2] = 1.0 - 2.0 * (host_k % 2)
    wk = jnp.asarray(wk)
    w = np.array(gll_weights)
    tile = 256 if half % 256 == 0 else half
    w2 = np.zeros((PAD, 1), np.float32)
    w2[:N2, 0] = (w[:, None] * w[None, :]).reshape(-1)
    w2 = jnp.asarray(w2)

    turn = 2.0 * np.pi / planes
    base = turn * (host_k[:, None] * np.arange(tile)[None, :] % planes)
    steps = turn * (host_k[:, None] * tile * np.arange(half // tile)[None, :] % planes)
    rotation = np.stack([np.cos(steps), np.sin(steps)], axis=2).reshape(count, -1)
    tables = tuple(jnp.asarray(t.astype(np.float32)) for t in (np.cos(base), np.sin(base), rotation))
    tables = tables + grads + (wk, w2)
    in_planes = np.arange(3 * planes // 8, 5 * planes // 8)
    arg = 2.0 * np.pi * ((host_k[:, None] * in_planes[None, :]) % planes) / planes
    profile = math.sqrt(count) / planes * np.stack([np.cos(arg).sum(1), -np.sin(arg).sum(1)])
    profile = np.concatenate([profile, np.zeros((6, count))])
    profile = profile.astype(np.float32).reshape(8, groups, modes).transpose(1, 0, 2)
    tables = (jnp.asarray(profile),) + tables
    result = window(velocity, (column_width, row_height, disc_mask), tables, groups)
    return result.reshape(3, nodes, 2, modes)


def solution(mesh):
    return jax.shard_map(
        on_device,
        mesh=mesh,
        in_specs=(P(None, "elem", None, "mode"), P("elem"), P(), P("elem")),
        out_specs=P(None, "elem", None, "mode"),
        check_vma=False,
    )
```
